32 devices in a mesh: row: 4 (over x, core), col: 8 (over z, y).
Axes of the slice: x: 2, y: 2, z: 4, core: 2. Of those that a mesh axis runs over, the one named last changes fastest.
Arguments:
- currents: float32 [3, 131072], P(None, ('row', 'col')), may hold values from -6 to 6
- probes: float32 [3, 131072], P(None, ('row', 'col')), may hold values from -6 to 6
- proj_weights: float32 [4, 131072], P(None, ('row', 'col')), may hold values from 0.5 to 2
- interp_weights: float32 [4, 131072], P(None, ('row', 'col')), may hold values from 0.5 to 2
- owner: int32 [131072, 1], P(('row', 'col')), may hold values from 0 to 31; in each aligned block of 4096 rows (0 to 4095, 4096 to 8191, ...) at most 256 rows name the same one
- cell: int32 [131072], P(('row', 'col')), may hold values from 0 to 129023
- near_list: int32 [1024, 4], P(('row', 'col')), may hold values from 0 to 31
- near_matrix: bfloat16 [1024, 4, 128, 128], P(('row', 'col')), may hold values from -0.25 to 0.25
- kernel_hat: float32 [1, 2048, 2048], P(None, ('row', 'col')), as said below
Outputs:
- forward_out: float32 [3, 131072], P(None, ('row', 'col'))
- adjoint_out: float32 [3, 131072], P(None, ('row', 'col'))
The draws below stay inside these ranges and needn't reach their ends.
Inputs may be any that keep to these rules, and one draw needn't show every extreme that they name: Among the 4096 elements of one device no owner is named more than 256 times; in every draw some device names some owner exactly 256 times. Every entry is positive, and kernel_hat[t, ky, kx] equals kernel_hat[t, (2048 - ky) mod 2048, (2048 - kx) mod 2048].
All inputs are finite; a program needn't handle non-finite values.
Results may differ from the reference program's by a relative error of at most 0.0003.
Values sent between devices are 32-bit elements; how exact they have to be, the bound alone decides.
No kernel may reach another device: no remote copies, remote signals or barrier semaphores. Data moves between devices by JAX's collectives and lax.ppermute only.
A program may use at most 320 MiB of HBM per device.

```python
import math
import jax
import jax.numpy as jnp
import numpy as np
from jax import lax

NX = 2048
NY = 2048
PL = 1
E_DEV = 4096
BLOCK = 128
NEAR = 4
DZ = 1
ELEMS = 131072
CAP = 256
XROWS = 64
N_ROW = 4
N_COL = 8


def draw_kernel_hat(key, part):
    freq_y = jnp.arange(NY, dtype=jnp.float32)
    freq_x = jnp.arange(NX, dtype=jnp.float32)
    sine_y = jnp.sin(math.pi * freq_y / NY)
    sine_x = jnp.sin(math.pi * freq_x / NX)
    symbol = 4.0 * (sine_y * sine_y)[:, None] + 4.0 * (sine_x * sine_x)[None, :]
    wave = jnp.sqrt(symbol + 1e-06)
    offsets = jnp.abs(jnp.arange(DZ, dtype=jnp.float32) - (PL - 1))
    base = jnp.exp(-offsets[:, None, None] * wave[None, :, :]) * (0.5 + 1.0 / wave[None, :, :])
    rough = jax.random.uniform(key, (DZ, NY, NX), jnp.float32, 0.5, 1.5)
    mirrored = jnp.roll(jnp.flip(rough, axis=(1, 2)), 1, axis=(1, 2))
    return (0.5 * (rough + mirrored) * base).astype(jnp.float32)


def plant(result, key, least, largest):
    longest = result.shape.index(max(result.shape))
    spots = []
    for shift in (0, 1):
        where = [jax.random.randint(jax.random.fold_in(key, axis), (), 0, length) for axis, length in enumerate(result.shape)]
        where[longest] = (where[longest] + shift) % result.shape[longest]
        spots.append(tuple(where))
    return result.at[spots[0]].set(least).at[spots[1]].set(largest)


def levels(stream_key, shape, split, low, top_value):
    gain, own = 1.0, jax.random.fold_in(stream_key, 6)
    for dim, blocks in split:
        heights = jnp.exp(jax.random.uniform(jax.random.fold_in(own, dim), (blocks,), jnp.float32, low / len(split), top_value / len(split)))
        gain = gain * jnp.repeat(heights, shape[dim] // blocks).reshape([-1 if axis == dim else 1 for axis in range(len(shape))])
    return gain


def assign_block(rng, own, number, rows, number_of, top, most, slope):
    ranking = jax.random.permutation(rng, number_of)
    heavy_load, common = shares(number_of, rows * top, most, slope, True), shares(number_of, rows * top, most, slope, False)
    places = jnp.arange(number_of)

    def named(tallies, offset_by):
        used = int((tallies > 0).sum())
        fixed = max(1, used // 4)
        passed = fixed + (places - fixed + offset_by * (used - fixed)) % max(1, number_of - fixed)
        return jnp.zeros((number_of,), jnp.int32).at[ranking[jnp.where(places < fixed, places, passed)]].set(jnp.asarray(tallies, jnp.int32))

    tallies = jnp.where(number % 4 == 0, named(heavy_load, number // 4), named(common, number - number // 4 - 1))
    mixed = jax.random.permutation(jax.random.fold_in(own, 3), number_of)
    donor, taker = mixed[0:number_of // 2 * 2:2], mixed[1:number_of // 2 * 2:2]
    margin = jnp.minimum(tallies[donor] - 1, most - tallies[taker]) // 2
    margin = jnp.where((donor == ranking[0]) | (taker == ranking[0]) | (tallies[taker] == 0), 0, jnp.maximum(margin, 0))
    passed = jax.random.randint(jax.random.fold_in(own, 4), (number_of // 2,), 0, 1 << 20) % (margin + 1)
    tallies = tallies.at[donor].add(-passed).at[taker].add(passed)
    labels = jnp.searchsorted(jnp.cumsum(tallies), jnp.arange(rows * top), side="right").astype(jnp.int32)
    grid = labels.reshape(top, rows).T
    grid = grid[jax.random.permutation(jax.random.fold_in(own, 1), rows)]
    offset_by = jax.random.randint(jax.random.fold_in(own, 2), (rows, 1), 0, top)
    return jnp.take_along_axis(grid, (jnp.arange(top)[None, :] + offset_by) % top, axis=1)


def shares(amount, total, reach, skew, full):
    weights = [(1 << 20) // math.isqrt(standing ** skew) + 1 for standing in range(1, amount + 1)]
    largest = reach if full else min(reach, max(-(-total // amount), total * weights[0] // sum(weights)))
    least = 1 if total - largest >= amount - 1 else 0
    given, surplus = [largest] + [least] * (amount - 1), total - largest - least * (amount - 1)
    while surplus > 0:
        candidates = [i for i in range(1, amount) if given[i] < largest] or [i for i in range(1, amount) if given[i] < reach]
        mass, left = sum([weights[i] for i in candidates]), surplus
        for i in candidates:
            extra = min(reach - given[i], max(1, left * weights[i] // mass), surplus)
            given[i] = given[i] + extra
            surplus = surplus - extra
    return np.array(given)


def gaussian(rng, shape, scale, reach, pieces=(), kind=jnp.bfloat16):
    drawn = scale * jax.random.normal(rng, shape, jnp.float32)
    if pieces:
        drawn = drawn * levels(rng, shape, pieces, -0.22, 0.18)
    return jnp.clip(drawn, -reach, reach).astype(kind)


def setup_inputs(seed: int = 0) -> dict:
    keys = jax.random.split(jax.random.key(seed), 10)
    currents = gaussian(keys[0], (3, ELEMS), 1.0, 6.0, ((1, 32),), jnp.float32)
    probes = gaussian(keys[1], (3, ELEMS), 1.0, 6.0, ((1, 32),), jnp.float32)
    proj_weights = jnp.clip(jnp.exp(math.log(2.0) - 1.3862944 * jax.random.uniform(keys[2], (4, ELEMS), jnp.float32) ** levels(keys[2], (4, ELEMS), ((1, 32),), -0.2, 0.2)), 0.5, 2.0)
    interp_weights = jnp.clip(jnp.exp(math.log(2.0) - 1.3862944 * jax.random.uniform(keys[3], (4, ELEMS), jnp.float32) ** levels(keys[3], (4, ELEMS), ((1, 32),), -0.2, 0.2)), 0.5, 2.0)
    owner_keys = jax.random.split(jax.random.fold_in(keys[4], 1), ELEMS // E_DEV)
    owner_turns = jax.random.permutation(jax.random.fold_in(keys[4], 3), ELEMS // E_DEV)
    owner = jax.vmap(lambda own, number: assign_block(jax.random.fold_in(keys[4], 2), own, number, E_DEV, N_ROW * N_COL, 1, CAP, 2))(owner_keys, owner_turns).reshape((ELEMS, 1))
    cell = plant(jax.random.randint(keys[5], (ELEMS,), 0, PL * (XROWS - 1) * NY), jax.random.fold_in(keys[5], 1), 0, (PL * (XROWS - 1) * NY) - 1).astype(jnp.int32)
    near_list = plant(jax.random.randint(keys[6], (ELEMS // BLOCK, NEAR), 0, E_DEV // BLOCK), jax.random.fold_in(keys[6], 1), 0, (E_DEV // BLOCK) - 1).astype(jnp.int32)
    near_matrix = gaussian(keys[7], (ELEMS // BLOCK, NEAR, BLOCK, BLOCK), (NEAR * BLOCK) ** -0.5, 0.25, ((0, 32),))
    kernel_hat = draw_kernel_hat(jax.random.fold_in(keys[9], 71), 0)
    return {"currents": currents, "probes": probes, "proj_weights": proj_weights, "interp_weights": interp_weights, "owner": owner, "cell": cell, "near_list": near_list, "near_matrix": near_matrix, "kernel_hat": kernel_hat}


def near_terms(packed):
    cur_dev, probe_dev, list_dev, matrix_dev = packed
    matrices = matrix_dev.astype(jnp.float32)
    gathered = cur_dev[:, list_dev]
    forward_near = jnp.einsum('cbnj,bnij->cbi', gathered, matrices, precision=lax.Precision.HIGHEST)
    spread_back = jnp.einsum('cbi,bnij->cbnj', probe_dev, matrices, precision=lax.Precision.HIGHEST)
    adjoint_near = jnp.zeros_like(probe_dev).at[:, list_dev].add(spread_back)
    return forward_near, adjoint_near


def reference(currents, probes, proj_weights, interp_weights, owner, cell, near_list, near_matrix, kernel_hat):
    devices = N_ROW * N_COL
    x_local = NX // devices
    target = owner[:, 0]
    plane_of = cell // ((x_local - 1) * NY)
    row_of = (cell // NY) % (x_local - 1)
    col_of = cell % NY
    grid_row = target * x_local + row_of
    cells_list = []
    for shift_x in range(2):
        for shift_y in range(2):
            cells_list.append(plane_of * (NX * NY) + (grid_row + shift_x) * NY + (col_of + shift_y) % NY)
    stencil = jnp.stack(cells_list).astype(jnp.int32)
    kernel_xy = jnp.transpose(kernel_hat, (0, 2, 1))
    outputs = []
    for field_index in range(6):
        if field_index < 3:
            values = currents[field_index][None, :] * proj_weights
            weights = interp_weights
        else:
            values = probes[field_index - 3][None, :] * interp_weights
            weights = proj_weights
        grid_vals = jnp.zeros((PL * NX * NY,), jnp.float32).at[stencil.reshape(-1)].add(values.reshape(-1))
        spectrum = jnp.fft.fft2(grid_vals.reshape(PL, NX, NY))
        mixed_list = []
        for target_plane in range(PL):
            total = kernel_xy[target_plane + PL - 1] * spectrum[0]
            for source_plane in range(1, PL):
                total = total + kernel_xy[target_plane - source_plane + PL - 1] * spectrum[source_plane]
            mixed_list.append(total)
        potential = jnp.real(jnp.fft.ifft2(jnp.stack(mixed_list))).reshape(-1)
        samples = potential[stencil]
        outputs.append(jnp.sum(samples * weights, axis=0))
    blocks = E_DEV // BLOCK
    cur_dev = jnp.transpose(currents.reshape(3, devices, blocks, BLOCK), (1, 0, 2, 3))
    probe_dev = jnp.transpose(probes.reshape(3, devices, blocks, BLOCK), (1, 0, 2, 3))
    list_dev = near_list.reshape(devices, blocks, NEAR)
    matrix_dev = near_matrix.reshape(devices, blocks, NEAR, BLOCK, BLOCK)
    forward_near, adjoint_near = lax.map(near_terms, (cur_dev, probe_dev, list_dev, matrix_dev))
    forward_near = jnp.transpose(forward_near, (1, 0, 2, 3)).reshape(3, devices * E_DEV)
    adjoint_near = jnp.transpose(adjoint_near, (1, 0, 2, 3)).reshape(3, devices * E_DEV)
    forward_out = jnp.stack(outputs[0:3]) + forward_near
    adjoint_out = jnp.stack(outputs[3:6]) + adjoint_near
    return forward_out, adjoint_out
```

```python
import math

import jax
import jax.numpy as jnp
import numpy as np
from jax import lax
from jax.experimental import pallas as pl
from jax.experimental.pallas import tpu as pltpu
from jax.sharding import PartitionSpec as P

AXES = ("row", "col")
LANES = 128
HALVES = 2
F32 = jnp.float32
BF16 = jnp.bfloat16
NT = (((1,), (1,)), ((), ()))
NN = (((1,), (0,)), ((), ()))


def split_np(table):
    hi = table.astype(np.float32).astype(jnp.bfloat16)
    lo = (table - hi.astype(np.float64)).astype(np.float32).astype(jnp.bfloat16)
    return jnp.asarray(hi), jnp.asarray(lo)


def split(x):
    hi = x.astype(BF16)
    return hi, (x - hi.astype(F32)).astype(BF16)


def dot(a, b, dims):
    return lax.dot_general(a, b, dims, preferred_element_type=F32)


def dot3(a, b, dims):
    (ah, al), (bh, bl) = a, b
    return dot(ah, bh, dims) + (dot(ah, bl, dims) + dot(al, bh, dims))


def y_table(devices, per):
    d, c, h, q, hh, cc, y = np.ix_(
        range(devices), range(2), range(HALVES), range(per), range(HALVES), range(2), range(LANES)
    )
    angle = 2.0 * math.pi * (((d * per + q) * y) % LANES) / LANES
    sine = np.where(c < cc, 1.0, -1.0) * np.sin(angle)
    value = np.where(c == cc, np.cos(angle), sine) * (h == hh)
    return value.reshape(devices * 2 * HALVES * per, HALVES * 2 * LANES)


def x_table(length, direction):
    copies = LANES // length
    c, p, x, cc, pp, k = np.ix_(
        range(2), range(copies), range(length), range(2), range(copies), range(length)
    )
    angle = direction * 2.0 * math.pi * ((x * k) % length) / length
    sine = np.where(c < cc, 1.0, -1.0) * np.sin(angle)
    value = np.where(c == cc, np.cos(angle), sine) * (p == pp)
    return value.reshape(2 * LANES, 2 * LANES)


def phases(rows, cols, length):
    turns = (np.arange(rows)[:, None] * np.arange(cols)[None, :]) % length
    angle = 2.0 * math.pi * turns / length
    return np.cos(angle), np.sin(angle)


def fft_list(re, im, direction):
    n = len(re)
    if n == 1:
        return re, im
    even_re, even_im = fft_list(re[0::2], im[0::2], direction)
    odd_re, odd_im = fft_list(re[1::2], im[1::2], direction)
    low_re, low_im, high_re, high_im = [], [], [], []
    for k in range(n // 2):
        a, b = odd_re[k], odd_im[k]
        if k == 0:
            tr, ti = a, b
        elif 4 * k == n:
            tr, ti = (-b, a) if direction > 0 else (b, -a)
        else:
            cos = math.cos(2.0 * math.pi * k / n)
            sin = direction * math.sin(2.0 * math.pi * k / n)
            tr, ti = a * cos - b * sin, a * sin + b * cos
        low_re.append(even_re[k] + tr)
        low_im.append(even_im[k] + ti)
        high_re.append(even_re[k] - tr)
        high_im.append(even_im[k] - ti)
    return low_re + high_re, low_im + high_im


def one_hot(cols, start, size):
    ids = lax.broadcasted_iota(jnp.int32, (size, cols.shape[1]), 0) + start
    return jnp.where(ids == cols, 1.0, 0.0).astype(BF16)


def project_call(field, rc, payload, yhi, ylo, tw_cos, tw_sin, x_local, grid_y):
    slots = rc.shape[1]
    n1 = grid_y // LANES
    k1l = n1 // HALVES
    rows = k1l * x_local
    width = HALVES * 2 * LANES
    build = 512
    wide = 1024
    window = 256

    def kernel(rc_ref, pay_ref, yhi_ref, ylo_ref, cos_ref, sin_ref, out_ref, v_ref, g0_ref, g1_ref, x_ref):
        half = 4 * x_local

        @pl.loop(0, slots // build)
        def _(i):
            at = pl.ds(pl.multiple_of(i * build, build), build)
            row = rc_ref[0:1, at]
            ids = lax.broadcasted_iota(jnp.int32, (x_local, build), 0)
            m0 = ids == row
            m1 = ids == row + 1
            for c in range(2):
                u = pay_ref[3 * c + field : 3 * c + field + 1, at]
                for b in range(2):
                    p0 = u * pay_ref[6 + 4 * c + b : 7 + 4 * c + b, at]
                    p1 = u * pay_ref[8 + 4 * c + b : 9 + 4 * c + b, at]
                    value = jnp.where(m0, p0, jnp.where(m1, p1, 0.0))
                    hi, lo = split(value)
                    base = (b * 2 + c) * x_local
                    v_ref[base : base + x_local, at] = hi
                    v_ref[half + base : half + base + x_local, at] = lo

        @pl.loop(0, grid_y // window)
        def _(w):
            start = pl.multiple_of(w * window, window)

            def step(i, acc):
                at = pl.ds(pl.multiple_of(i * wide, wide), wide)
                hot = one_hot(rc_ref[1:2, at], start, window)
                return acc + dot(v_ref[:, at], hot, NT)

            acc = lax.fori_loop(0, slots // wide, step, jnp.zeros((2 * half, window), F32))
            total = acc[:half] + acc[half:]
            g0_ref[:, pl.ds(start, window)] = total[: 2 * x_local]
            g1_ref[:, pl.ds(start, window)] = total[2 * x_local :]

        g0_ref[...] = g0_ref[...] + pltpu.roll(g1_ref[...], 1, 1)

        @pl.loop(0, x_local // 8)
        def _(i):
            re_at = pl.ds(pl.multiple_of(i * 8, 8), 8)
            im_at = pl.ds(pl.multiple_of(x_local + i * 8, 8), 8)
            re = [g0_ref[re_at, y * LANES : (y + 1) * LANES] for y in range(n1)]
            im = [g0_ref[im_at, y * LANES : (y + 1) * LANES] for y in range(n1)]
            re, im = fft_list(re, im, -1.0)
            for k in range(n1):
                cos, sin = cos_ref[k : k + 1, :], sin_ref[k : k + 1, :]
                to = pl.ds(pl.multiple_of((k % k1l) * x_local + i * 8, 8), 8)
                left = (k // k1l) * 2 * LANES
                x_ref[to, left : left + LANES] = re[k] * cos + im[k] * sin
                x_ref[to, left + LANES : left + 2 * LANES] = im[k] * cos - re[k] * sin

        out_ref[...] = dot3((yhi_ref[...], ylo_ref[...]), split(x_ref[...]), NT)

    return pl.pallas_call(
        kernel,
        out_shape=jax.ShapeDtypeStruct((yhi.shape[0], rows), F32),
        scratch_shapes=[
            pltpu.VMEM((8 * x_local, slots), BF16),
            pltpu.VMEM((2 * x_local, grid_y), F32),
            pltpu.VMEM((2 * x_local, grid_y), F32),
            pltpu.VMEM((rows, width), F32),
        ],
        compiler_params=pltpu.CompilerParams(vmem_limit_bytes=48 << 20),
        name="project",
    )(rc, payload, yhi, ylo, tw_cos, tw_sin)


def spectral_call(data, kernel_t, fwd, inv, tw_cos, tw_sin, devices):
    lanes = data.shape[1]
    rows = data.shape[0] // (2 * devices)

    def kernel(in_ref, kt_ref, fh_ref, fl_ref, ih_ref, il_ref, cos_ref, sin_ref, out_ref, re_ref, im_ref):
        @pl.loop(0, lanes // LANES)
        def _(t):
            at = pl.ds(pl.multiple_of(t * LANES, LANES), LANES)
            re = [in_ref[(2 * s) * rows : (2 * s + 1) * rows, at] for s in range(devices)]
            im = [in_ref[(2 * s + 1) * rows : (2 * s + 2) * rows, at] for s in range(devices)]
            re, im = fft_list(re, im, -1.0)
            for k in range(devices):
                cos, sin = cos_ref[k : k + 1, at], sin_ref[k : k + 1, at]
                re_ref[k * rows : (k + 1) * rows, at] = re[k] * cos + im[k] * sin
                im_ref[k * rows : (k + 1) * rows, at] = im[k] * cos - re[k] * sin

        for t in range(lanes // LANES):
            at = slice(t * LANES, (t + 1) * LANES)
            both = jnp.concatenate([re_ref[:, at], im_ref[:, at]], axis=1)
            spectrum = dot3(split(both), (fh_ref[...], fl_ref[...]), NN)
            factor = kt_ref[:, at]
            both = jnp.concatenate([spectrum[:, :LANES] * factor, spectrum[:, LANES:] * factor], axis=1)
            back = dot3(split(both), (ih_ref[...], il_ref[...]), NN)
            re_ref[:, at] = back[:, :LANES]
            im_ref[:, at] = back[:, LANES:]

        @pl.loop(0, lanes // LANES)
        def _(t):
            at = pl.ds(pl.multiple_of(t * LANES, LANES), LANES)
            re, im = [], []
            for k in range(devices):
                cos, sin = cos_ref[k : k + 1, at], sin_ref[k : k + 1, at]
                a = re_ref[k * rows : (k + 1) * rows, at]
                b = im_ref[k * rows : (k + 1) * rows, at]
                re.append(a * cos - b * sin)
                im.append(b * cos + a * sin)
            re, im = fft_list(re, im, 1.0)
            for s in range(devices):
                out_ref[(2 * s) * rows : (2 * s + 1) * rows, at] = re[s]
                out_ref[(2 * s + 1) * rows : (2 * s + 2) * rows, at] = im[s]

    return pl.pallas_call(
        kernel,
        out_shape=jax.ShapeDtypeStruct(data.shape, F32),
        scratch_shapes=[
            pltpu.VMEM((devices * rows, lanes), F32),
            pltpu.VMEM((devices * rows, lanes), F32),
        ],
        compiler_params=pltpu.CompilerParams(vmem_limit_bytes=48 << 20),
        name="spectral",
    )(data, kernel_t, *fwd, *inv, tw_cos, tw_sin)


def sample_call(data, rc, payload, yhi, ylo, tw_cos, tw_sin, x_local, grid_y):
    slots = rc.shape[1]
    n1 = grid_y // LANES
    k1l = n1 // HALVES
    rows = k1l * x_local
    width = HALVES * 2 * LANES
    block = 256

    def kernel(in_ref, rc_ref, pay_ref, yhi_ref, ylo_ref, cos_ref, sin_ref, out_ref, u_ref, g_ref, p_ref):
        half = 4 * x_local
        turned = jnp.transpose(in_ref[...])
        u_ref[...] = dot3(split(turned), (yhi_ref[...], ylo_ref[...]), NN)

        @pl.loop(0, x_local // 8)
        def _(i):
            re, im = [], []
            for k in range(n1):
                cos, sin = cos_ref[k : k + 1, :], sin_ref[k : k + 1, :]
                at = pl.ds(pl.multiple_of((k % k1l) * x_local + i * 8, 8), 8)
                left = (k // k1l) * 2 * LANES
                a = u_ref[at, left : left + LANES]
                b = u_ref[at, left + LANES : left + 2 * LANES]
                re.append(a * cos - b * sin)
                im.append(b * cos + a * sin)
            re, im = fft_list(re, im, 1.0)
            re_at = pl.ds(pl.multiple_of(i * 8, 8), 8)
            im_at = pl.ds(pl.multiple_of(x_local + i * 8, 8), 8)
            for y in range(n1):
                g_ref[re_at, y * LANES : (y + 1) * LANES] = re[y]
                g_ref[im_at, y * LANES : (y + 1) * LANES] = im[y]

        hi, lo = split(g_ref[...])
        p_ref[0 : 2 * x_local] = hi
        p_ref[half : half + 2 * x_local] = lo
        hi, lo = split(pltpu.roll(g_ref[...], grid_y - 1, 1))
        p_ref[2 * x_local : half] = hi
        p_ref[half + 2 * x_local :] = lo

        @pl.loop(0, slots // block)
        def _(i):
            at = pl.ds(pl.multiple_of(i * block, block), block)
            hot = one_hot(rc_ref[1:2, at], 0, grid_y)
            both = dot(p_ref[...], hot, NN)
            total = both[:half] + both[half:]
            row = rc_ref[0:1, at]
            ids = lax.broadcasted_iota(jnp.int32, (x_local, block), 0)
            m0 = ids == row
            m1 = ids == row + 1
            for c in range(2):
                result = jnp.zeros((x_local, block), F32)
                for b in range(2):
                    other = 10 - 4 * c
                    w0 = pay_ref[other + b : other + b + 1, at]
                    w1 = pay_ref[other + 2 + b : other + 3 + b, at]
                    base = (b * 2 + c) * x_local
                    weight = jnp.where(m0, w0, jnp.where(m1, w1, 0.0))
                    result = result + weight * total[base : base + x_local]
                out_ref[c : c + 1, at] = jnp.sum(result, axis=0, keepdims=True)

    return pl.pallas_call(
        kernel,
        out_shape=jax.ShapeDtypeStruct((2, slots), F32),
        scratch_shapes=[
            pltpu.VMEM((rows, width), F32),
            pltpu.VMEM((2 * x_local, grid_y), F32),
            pltpu.VMEM((8 * x_local, grid_y), BF16),
        ],
        compiler_params=pltpu.CompilerParams(vmem_limit_bytes=48 << 20),
        name="sample",
    )(data, rc, payload, yhi, ylo, tw_cos, tw_sin)


def near_terms(currents, probes, near_list, near_matrix):
    block_len = near_matrix.shape[2]
    blocks = near_list.shape[0]
    select = (near_list[:, :, None] == jnp.arange(blocks, dtype=jnp.int32)[None, None, :]).astype(F32)
    cur_blocks = currents.reshape(3, blocks, block_len)
    gathered = jnp.einsum("ctj,bnt->cbnj", cur_blocks, select, precision=lax.Precision.HIGHEST)
    g_hi, g_lo = split(gathered)
    forward = jnp.einsum(
        "cbnj,bnij->cbi", jnp.concatenate([g_hi, g_lo]), near_matrix, preferred_element_type=F32
    )
    p_hi, p_lo = split(probes.reshape(3, blocks, block_len))
    spread = jnp.einsum(
        "cbi,bnij->cbnj", jnp.concatenate([p_hi, p_lo]), near_matrix, preferred_element_type=F32
    )
    adjoint = jnp.einsum(
        "cbnj,bnt->ctj", spread[:3] + spread[3:], select, precision=lax.Precision.HIGHEST
    )
    return (forward[:3] + forward[3:]).reshape(3, -1), adjoint.reshape(3, -1)


def on_device(
    currents, probes, proj_weights, interp_weights, owner, cell, near_list, near_matrix, kernel_hat
):
    devices = lax.axis_size("row") * lax.axis_size("col")
    elem_count = currents.shape[1]
    capacity = 2 * elem_count // devices
    dz_count, ky_local, grid_x = kernel_hat.shape
    assert dz_count == 1
    grid_y = ky_local * devices
    x_local = grid_x // devices
    slots = devices * capacity
    n1 = grid_y // LANES
    per = ky_local // n1
    k1l = n1 // HALVES

    target = owner[:, 0]
    owner_ids = jnp.arange(devices, dtype=jnp.int32)
    member = (target[:, None] == owner_ids[None, :]).astype(jnp.int32)
    before = jnp.cumsum(member, axis=0) - member
    slot_index = jnp.sum(before * member, axis=1)
    position = target * capacity + slot_index
    payload = jnp.concatenate(
        [currents, probes, proj_weights, interp_weights, cell.astype(F32)[None, :]], axis=0
    )
    outgoing = jnp.zeros((15, slots), F32).at[:, position].set(payload)
    arrived = lax.all_to_all(
        outgoing.reshape(15, devices, capacity), AXES, split_axis=1, concat_axis=1, tiled=True
    ).reshape(15, slots)
    cell_in = arrived[14].astype(jnp.int32)
    rc = jnp.stack([cell_in // grid_y % (x_local - 1), cell_in % grid_y])

    yhi, ylo = split_np(y_table(devices, per))
    ty_cos, ty_sin = (jnp.asarray(t, F32) for t in phases(n1, LANES, grid_y))
    tx_cos, tx_sin = (
        jnp.asarray(np.tile(t, (1, k1l)), F32) for t in phases(devices, x_local, grid_x)
    )
    fwd, inv = split_np(x_table(x_local, -1.0)), split_np(x_table(x_local, 1.0))

    kernel_view = kernel_hat.reshape(per, HALVES, k1l, x_local, devices)
    kernel_t = jnp.transpose(kernel_view, (4, 1, 0, 2, 3)) * (1.0 / (grid_x * grid_y))
    kernel_t = kernel_t.reshape(devices * HALVES * per, k1l * x_local)

    def exchange(x):
        shaped = x.reshape(devices, 2 * HALVES * per, x.shape[1])
        moved = lax.all_to_all(shaped, AXES, split_axis=0, concat_axis=0, tiled=True)
        return moved.reshape(x.shape)

    results = []
    for field in range(3):
        spectra = project_call(
            field, rc, arrived, yhi, ylo, ty_cos, ty_sin, x_local, grid_y
        )
        spectra = exchange(spectra)
        products = spectral_call(spectra, kernel_t, fwd, inv, tx_cos, tx_sin, devices)
        products = exchange(products)
        results.append(
            sample_call(products, rc, arrived, yhi, ylo, ty_cos, ty_sin, x_local, grid_y)
        )
    stacked = jnp.concatenate(results, axis=0).reshape(6, devices, capacity)
    returned = lax.all_to_all(stacked, AXES, split_axis=1, concat_axis=1, tiled=True).reshape(6, slots)
    homed = returned[:, position]
    near_forward, near_adjoint = near_terms(currents, probes, near_list, near_matrix)
    return (homed[0::2] + near_forward, homed[1::2] + near_adjoint)


def solution(mesh):
    return jax.shard_map(
        on_device,
        mesh=mesh,
        in_specs=(
            P(None, AXES),
            P(None, AXES),
            P(None, AXES),
            P(None, AXES),
            P(AXES, None),
            P(AXES),
            P(AXES, None),
            P(AXES, None, None, None),
            P(None, AXES, None),
        ),
        out_specs=(P(None, AXES), P(None, AXES)),
        check_vma=False,
    )
```

```python
import math

import jax
import jax.numpy as jnp
import numpy as np
from jax import lax
from jax.experimental import pallas as pl
from jax.experimental.pallas import tpu as pltpu
from jax.sharding import PartitionSpec as P

AXES = ("row", "col")
LANES = 128
HALVES = 2
GROUP = 8
CHUNK = 512
WINDOW = 256
F32 = jnp.float32
BF16 = jnp.bfloat16
NT = (((1,), (1,)), ((), ()))
NN = (((1,), (0,)), ((), ()))


def split_np(table):
    hi = table.astype(np.float32).astype(jnp.bfloat16)
    lo = (table - hi.astype(np.float64)).astype(np.float32).astype(jnp.bfloat16)
    return jnp.asarray(hi), jnp.asarray(lo)


def split(x):
    hi = x.astype(BF16)
    return hi, (x - hi.astype(F32)).astype(BF16)


def dot(a, b, dims):
    return lax.dot_general(a, b, dims, preferred_element_type=F32)


def dot3(a, b, dims):
    (ah, al), (bh, bl) = a, b
    return dot(ah, bh, dims) + (dot(ah, bl, dims) + dot(al, bh, dims))


def y_table(devices, per):
    d, c, h, q, hh, cc, y = np.ix_(
        range(devices), range(2), range(HALVES), range(per), range(HALVES), range(2), range(LANES)
    )
    angle = 2.0 * math.pi * (((d * per + q) * y) % LANES) / LANES
    sine = np.where(c < cc, 1.0, -1.0) * np.sin(angle)
    value = np.where(c == cc, np.cos(angle), sine) * (h == hh)
    return value.reshape(devices * 2 * HALVES * per, HALVES * 2 * LANES)


def x_table(length, direction):
    copies = LANES // length
    c, p, x, cc, pp, k = np.ix_(
        range(2), range(copies), range(length), range(2), range(copies), range(length)
    )
    angle = direction * 2.0 * math.pi * ((x * k) % length) / length
    sine = np.where(c < cc, 1.0, -1.0) * np.sin(angle)
    value = np.where(c == cc, np.cos(angle), sine) * (p == pp)
    return value.reshape(2 * LANES, 2 * LANES)


def phases(rows, cols, length):
    turns = (np.arange(rows)[:, None] * np.arange(cols)[None, :]) % length
    angle = 2.0 * math.pi * turns / length
    return np.cos(angle), np.sin(angle)


def fft_list(re, im, direction):
    n = len(re)
    if n == 1:
        return re, im
    even_re, even_im = fft_list(re[0::2], im[0::2], direction)
    odd_re, odd_im = fft_list(re[1::2], im[1::2], direction)
    low_re, low_im, high_re, high_im = [], [], [], []
    for k in range(n // 2):
        a, b = odd_re[k], odd_im[k]
        if k == 0:
            tr, ti = a, b
        elif 4 * k == n:
            tr, ti = (-b, a) if direction > 0 else (b, -a)
        else:
            cos = math.cos(2.0 * math.pi * k / n)
            sin = direction * math.sin(2.0 * math.pi * k / n)
            tr, ti = a * cos - b * sin, a * sin + b * cos
        low_re.append(even_re[k] + tr)
        low_im.append(even_im[k] + ti)
        high_re.append(even_re[k] - tr)
        high_im.append(even_im[k] - ti)
    return low_re + high_re, low_im + high_im


def one_hot(cols, start, size):
    ids = lax.broadcasted_iota(jnp.int32, (size, cols.shape[1]), 0) + start
    return jnp.where(ids == cols, 1.0, 0.0).astype(BF16)


def call(kernel, name, out_shape, args, scratch=(), smem_in=(), smem_out=(), flops=0, after=()):
    if after:
        count, inner = len(args), kernel
        kernel = lambda *refs: inner(*refs[:count], *refs[count + len(after) :])
    spaces = [pltpu.SMEM if i in smem_in else pltpu.VMEM for i in range(len(args))]
    outs = [pltpu.SMEM if i in smem_out else pltpu.VMEM for i in range(len(out_shape))]
    moved = sum(math.prod(x.shape) * x.dtype.itemsize for x in (*args, *out_shape))
    return pl.pallas_call(
        kernel,
        out_shape=list(out_shape),
        in_specs=[pl.BlockSpec(memory_space=space) for space in spaces]
        + [pl.BlockSpec(memory_space=pl.ANY)] * len(after),
        out_specs=[pl.BlockSpec(memory_space=space) for space in outs],
        scratch_shapes=list(scratch),
        compiler_params=pltpu.CompilerParams(vmem_limit_bytes=48 << 20),
        cost_estimate=pl.CostEstimate(flops=flops, transcendentals=0, bytes_accessed=moved),
        name=name,
    )(*args, *after)


def shape(dims, dtype=F32):
    return jax.ShapeDtypeStruct(dims, dtype)


def expand_call(starts, keys, rows, devices, capacity, codes):
    count = keys.shape[1]
    wide = -(-capacity // LANES) * LANES + LANES
    height = 16

    def kernel(starts_ref, key_ref, *refs):
        row_refs, out_ref, s_ref = refs[:-2], refs[-2], refs[-1]
        s_ref[:, count:] = jnp.zeros((height, wide), F32)
        for i, ref in enumerate(row_refs):
            s_ref[i : i + 1, 0:count] = ref[...]
        s_ref[height - 1 : height, 0:count] = (key_ref[...] & (codes - 1)).astype(F32)
        lane = lax.broadcasted_iota(jnp.int32, (height, wide), 1)
        free = jnp.where(lax.broadcasted_iota(jnp.int32, (height, wide), 0) == height - 1, -1.0, 0.0)

        @pl.loop(0, devices)
        def _(d):
            first = starts_ref[d]
            held = starts_ref[d + 1] - first
            tile = first // LANES
            block = s_ref[:, pl.ds(pl.multiple_of(tile * LANES, LANES), wide)]
            moved = pltpu.roll(block, wide - (first - tile * LANES), 1)
            out_ref[d] = jnp.where(lane < held, moved, free)[:, :capacity]

    (out,) = call(
        kernel,
        "expand",
        [shape((devices, height, capacity))],
        [starts, keys, *rows],
        scratch=[pltpu.VMEM((height, count + wide), F32)],
        smem_in=(0,),
    )
    return out


def compact_call(starts, data, count):
    devices, height, capacity = data.shape
    wide = -(-capacity // LANES) * LANES + LANES

    def kernel(starts_ref, in_ref, out_ref, s_ref):
        lane = lax.broadcasted_iota(jnp.int32, (height, wide), 1)

        @pl.loop(0, devices)
        def _(d):
            first = starts_ref[d]
            held = starts_ref[d + 1] - first
            tile = first // LANES
            shift = first - tile * LANES
            at = pl.ds(pl.multiple_of(tile * LANES, LANES), wide)
            filler = jnp.zeros((height, wide - capacity), F32)
            moved = pltpu.roll(jnp.concatenate([in_ref[d], filler], axis=1), shift, 1)
            keep = (lane >= shift) & (lane < shift + held)
            s_ref[:, at] = jnp.where(keep, moved, s_ref[:, at])

        out_ref[...] = s_ref[:, :count]

    (out,) = call(
        kernel,
        "compact",
        [shape((height, count))],
        [starts, data],
        scratch=[pltpu.VMEM((height, count + wide), F32)],
        smem_in=(0,),
    )
    return out


def turn_blocks(parts):
    parts = list(parts)
    block = lax.broadcasted_iota(jnp.int32, parts[0].shape, 1) // GROUP
    for m in (1, 2, 4, 8):
        high = (block & m) != 0
        for i in range(16):
            if i & m == 0:
                a, b = parts[i], parts[i + m]
                parts[i] = jnp.where(high, pltpu.roll(b, m * GROUP, 1), a)
                parts[i + m] = jnp.where(high, b, pltpu.roll(a, LANES - m * GROUP, 1))
    return parts


def gather_groups(arrived, x_local, chunk):
    devices, height, capacity = arrived.shape
    slots = devices * capacity
    chunks = slots // chunk
    shift = x_local.bit_length() - 1
    none = 1 << 20

    def decode(code):
        return code & (x_local - 1), lax.shift_right_arithmetic(code, shift)

    if capacity % LANES or devices % 16:
        turned = arrived.reshape(devices, height, capacity // GROUP, GROUP)
        turned = jnp.transpose(turned, (1, 2, 0, 3)).reshape(height, slots)
        row, col = decode(turned[height - 1].astype(jnp.int32))
        per_chunk = col.reshape(chunks, chunk)
        low = jnp.min(jnp.where(per_chunk < 0, none, per_chunk), axis=1)
        return turned, jnp.stack([row, col]), jnp.stack([low, jnp.max(per_chunk, axis=1)])

    def kernel(in_ref, out_ref, rc_ref, bound_ref):
        @pl.loop(0, devices // 16)
        def _(sb):
            for t in range(capacity // LANES):
                lanes = slice(t * LANES, (t + 1) * LANES)
                parts = turn_blocks([in_ref[sb * 16 + i, :, lanes] for i in range(16)])
                for j in range(16):
                    left = (t * 16 + j) * devices * GROUP
                    at = pl.ds(pl.multiple_of(left + sb * LANES, LANES), LANES)
                    out_ref[:, at] = parts[j]
                    row, col = decode(parts[j][height - 1 :].astype(jnp.int32))
                    rc_ref[0:1, at] = row
                    rc_ref[1:2, at] = col

        @pl.loop(0, chunks)
        def _(i):
            col = rc_ref[1:2, pl.ds(pl.multiple_of(i * chunk, chunk), chunk)]
            bound_ref[0, i] = jnp.min(jnp.where(col < 0, none, col))
            bound_ref[1, i] = jnp.max(col)

    return call(
        kernel,
        "groups",
        [shape((height, slots)), shape((2, slots), jnp.int32), shape((2, chunks), jnp.int32)],
        [arrived],
        smem_out=(2,),
    )


def scatter_groups(results, devices, capacity):
    height = results.shape[0]
    if capacity % LANES or devices % 16:
        turned = results.reshape(height, capacity // GROUP, devices, GROUP)
        return jnp.transpose(turned, (2, 0, 1, 3)).reshape(devices, height, capacity)

    def kernel(in_ref, out_ref):
        @pl.loop(0, devices // 16)
        def _(sb):
            for t in range(capacity // LANES):
                parts = []
                for j in range(16):
                    left = (t * 16 + j) * devices * GROUP
                    parts.append(in_ref[:, pl.ds(pl.multiple_of(left + sb * LANES, LANES), LANES)])
                for i, part in enumerate(turn_blocks(parts)):
                    out_ref[sb * 16 + i, :, t * LANES : (t + 1) * LANES] = part

    (out,) = call(kernel, "ungroup", [shape((devices, height, capacity))], [results])
    return out


def window_count(bound_ref, i):
    first = bound_ref[0, i] // LANES
    return first, (bound_ref[1, i] - first * LANES) // WINDOW + 1


def project_call(field, bounds, rc, payload, yhi, ylo, tw_cos, tw_sin, x_local, grid_y, after):
    slots = rc.shape[1]
    chunks = bounds.shape[1]
    chunk = slots // chunks
    n1 = grid_y // LANES
    k1l = n1 // HALVES
    rows = k1l * x_local
    width = HALVES * 2 * LANES
    half = 4 * x_local

    def kernel(bound_ref, rc_ref, pay_ref, yhi_ref, ylo_ref, cos_ref, sin_ref, out_ref, v_ref, acc_ref, g_ref, x_ref):
        acc_ref[...] = jnp.zeros(acc_ref.shape, F32)

        @pl.loop(0, chunks)
        def _(i):
            at = pl.ds(pl.multiple_of(i * chunk, chunk), chunk)
            ids = lax.broadcasted_iota(jnp.int32, (x_local, chunk), 0)
            m0 = ids == rc_ref[0:1, at]
            m1 = ids == rc_ref[0:1, at] + 1
            for c in range(2):
                u = pay_ref[3 * c + field : 3 * c + field + 1, at]
                for b in range(2):
                    p0 = u * pay_ref[6 + 4 * c + b : 7 + 4 * c + b, at]
                    p1 = u * pay_ref[8 + 4 * c + b : 9 + 4 * c + b, at]
                    hi, lo = split(jnp.where(m0, p0, jnp.where(m1, p1, 0.0)))
                    base = (b * 2 + c) * x_local
                    v_ref[base : base + x_local, :] = hi
                    v_ref[half + base : half + base + x_local, :] = lo
            first, windows = window_count(bound_ref, i)

            def step(w, carry):
                start = first * LANES + w * WINDOW
                to = pl.ds(pl.multiple_of(start, LANES), WINDOW)
                acc_ref[:, to] += dot(v_ref[...], one_hot(rc_ref[1:2, at], start, WINDOW), NT)
                return carry

            lax.fori_loop(0, windows, step, 0)

        total = acc_ref[:half, :grid_y] + acc_ref[half:, :grid_y]
        g_ref[...] = total[: 2 * x_local] + pltpu.roll(total[2 * x_local :], 1, 1)

        @pl.loop(0, x_local // 8)
        def _(i):
            re_at = pl.ds(pl.multiple_of(i * 8, 8), 8)
            im_at = pl.ds(pl.multiple_of(x_local + i * 8, 8), 8)
            re = [g_ref[re_at, y * LANES : (y + 1) * LANES] for y in range(n1)]
            im = [g_ref[im_at, y * LANES : (y + 1) * LANES] for y in range(n1)]
            re, im = fft_list(re, im, -1.0)
            for k in range(n1):
                cos, sin = cos_ref[k : k + 1, :], sin_ref[k : k + 1, :]
                to = pl.ds(pl.multiple_of((k % k1l) * x_local + i * 8, 8), 8)
                left = (k // k1l) * 2 * LANES
                x_ref[to, left : left + LANES] = re[k] * cos + im[k] * sin
                x_ref[to, left + LANES : left + 2 * LANES] = im[k] * cos - re[k] * sin

        out_ref[...] = dot3((yhi_ref[...], ylo_ref[...]), split(x_ref[...]), NT)

    (out,) = call(
        kernel,
        "project",
        [shape((yhi.shape[0], rows))],
        [bounds, rc, payload, yhi, ylo, tw_cos, tw_sin],
        scratch=[
            pltpu.VMEM((2 * half, chunk), BF16),
            pltpu.VMEM((2 * half, grid_y + WINDOW), F32),
            pltpu.VMEM((2 * x_local, grid_y), F32),
            pltpu.VMEM((rows, width), F32),
        ],
        smem_in=(0,),
        flops=4 * half * slots * grid_y,
        after=after,
    )
    return out


def spectral_call(data, kernel_t, fwd, inv, tw_cos, tw_sin, devices, after):
    lanes = data.shape[1]
    rows = data.shape[0] // (2 * devices)

    def kernel(in_ref, kt_ref, fh_ref, fl_ref, ih_ref, il_ref, cos_ref, sin_ref, out_ref, re_ref, im_ref):
        @pl.loop(0, lanes // LANES)
        def _(t):
            at = pl.ds(pl.multiple_of(t * LANES, LANES), LANES)
            re = [in_ref[(2 * s) * rows : (2 * s + 1) * rows, at] for s in range(devices)]
            im = [in_ref[(2 * s + 1) * rows : (2 * s + 2) * rows, at] for s in range(devices)]
            re, im = fft_list(re, im, -1.0)
            for k in range(devices):
                cos, sin = cos_ref[k : k + 1, at], sin_ref[k : k + 1, at]
                re_ref[k * rows : (k + 1) * rows, at] = re[k] * cos + im[k] * sin
                im_ref[k * rows : (k + 1) * rows, at] = im[k] * cos - re[k] * sin

        for t in range(lanes // LANES):
            at = slice(t * LANES, (t + 1) * LANES)
            both = jnp.concatenate([re_ref[:, at], im_ref[:, at]], axis=1)
            spectrum = dot3(split(both), (fh_ref[...], fl_ref[...]), NN)
            factor = kt_ref[:, at]
            both = jnp.concatenate([spectrum[:, :LANES] * factor, spectrum[:, LANES:] * factor], axis=1)
            back = dot3(split(both), (ih_ref[...], il_ref[...]), NN)
            re_ref[:, at] = back[:, :LANES]
            im_ref[:, at] = back[:, LANES:]

        @pl.loop(0, lanes // LANES)
        def _(t):
            at = pl.ds(pl.multiple_of(t * LANES, LANES), LANES)
            re, im = [], []
            for k in range(devices):
                cos, sin = cos_ref[k : k + 1, at], sin_ref[k : k + 1, at]
                a = re_ref[k * rows : (k + 1) * rows, at]
                b = im_ref[k * rows : (k + 1) * rows, at]
                re.append(a * cos - b * sin)
                im.append(b * cos + a * sin)
            re, im = fft_list(re, im, 1.0)
            for s in range(devices):
                out_ref[(2 * s) * rows : (2 * s + 1) * rows, at] = re[s]
                out_ref[(2 * s + 1) * rows : (2 * s + 2) * rows, at] = im[s]

    (out,) = call(
        kernel,
        "spectral",
        [shape(data.shape)],
        [data, kernel_t, *fwd, *inv, tw_cos, tw_sin],
        scratch=[
            pltpu.VMEM((devices * rows, lanes), F32),
            pltpu.VMEM((devices * rows, lanes), F32),
        ],
        flops=1 << 30,
        after=after,
    )
    return out


def sample_call(data, bounds, rc, payload, yhi, ylo, tw_cos, tw_sin, x_local, grid_y, after):
    slots = rc.shape[1]
    n1 = grid_y // LANES
    k1l = n1 // HALVES
    rows = k1l * x_local
    width = HALVES * 2 * LANES
    chunks = bounds.shape[1]
    chunk = slots // chunks
    half = 4 * x_local

    def kernel(in_ref, bound_ref, rc_ref, pay_ref, yhi_ref, ylo_ref, cos_ref, sin_ref, out_ref, u_ref, g_ref, p_ref, t_ref):
        turned = jnp.transpose(in_ref[...])
        u_ref[...] = dot3(split(turned), (yhi_ref[...], ylo_ref[...]), NN)

        @pl.loop(0, x_local // 8)
        def _(i):
            re, im = [], []
            for k in range(n1):
                cos, sin = cos_ref[k : k + 1, :], sin_ref[k : k + 1, :]
                at = pl.ds(pl.multiple_of((k % k1l) * x_local + i * 8, 8), 8)
                left = (k // k1l) * 2 * LANES
                a = u_ref[at, left : left + LANES]
                b = u_ref[at, left + LANES : left + 2 * LANES]
                re.append(a * cos - b * sin)
                im.append(b * cos + a * sin)
            re, im = fft_list(re, im, 1.0)
            re_at = pl.ds(pl.multiple_of(i * 8, 8), 8)
            im_at = pl.ds(pl.multiple_of(x_local + i * 8, 8), 8)
            for y in range(n1):
                g_ref[re_at, y * LANES : (y + 1) * LANES] = re[y]
                g_ref[im_at, y * LANES : (y + 1) * LANES] = im[y]

        hi, lo = split(g_ref[...])
        p_ref[0 : 2 * x_local, :grid_y] = hi
        p_ref[half : half + 2 * x_local, :grid_y] = lo
        hi, lo = split(pltpu.roll(g_ref[...], grid_y - 1, 1))
        p_ref[2 * x_local : half, :grid_y] = hi
        p_ref[half + 2 * x_local :, :grid_y] = lo
        p_ref[:, grid_y:] = jnp.zeros((2 * half, WINDOW), BF16)

        @pl.loop(0, chunks)
        def _(i):
            at = pl.ds(pl.multiple_of(i * chunk, chunk), chunk)
            first, windows = window_count(bound_ref, i)
            t_ref[...] = jnp.zeros(t_ref.shape, F32)

            def step(w, carry):
                start = first * LANES + w * WINDOW
                of = pl.ds(pl.multiple_of(start, LANES), WINDOW)
                t_ref[...] += dot(p_ref[:, of], one_hot(rc_ref[1:2, at], start, WINDOW), NN)
                return carry

            lax.fori_loop(0, windows, step, 0)
            total = t_ref[:half] + t_ref[half:]
            ids = lax.broadcasted_iota(jnp.int32, (x_local, chunk), 0)
            m0 = ids == rc_ref[0:1, at]
            m1 = ids == rc_ref[0:1, at] + 1
            for c in range(2):
                result = jnp.zeros((x_local, chunk), F32)
                for b in range(2):
                    other = 10 - 4 * c
                    w0 = pay_ref[other + b : other + b + 1, at]
                    w1 = pay_ref[other + 2 + b : other + 3 + b, at]
                    base = (b * 2 + c) * x_local
                    weight = jnp.where(m0, w0, jnp.where(m1, w1, 0.0))
                    result = result + weight * total[base : base + x_local]
                out_ref[c : c + 1, at] = jnp.sum(result, axis=0, keepdims=True)

    (out,) = call(
        kernel,
        "sample",
        [shape((2, slots))],
        [data, bounds, rc, payload, yhi, ylo, tw_cos, tw_sin],
        scratch=[
            pltpu.VMEM((rows, width), F32),
            pltpu.VMEM((2 * x_local, grid_y), F32),
            pltpu.VMEM((2 * half, grid_y + WINDOW), BF16),
            pltpu.VMEM((2 * half, chunk), F32),
        ],
        smem_in=(1,),
        flops=4 * half * slots * grid_y,
        after=after,
    )
    return out


def split_outside(x):
    hi = lax.reduce_precision(x, 8, 7)
    return hi.astype(BF16), (x - hi).astype(BF16)


def near_terms(currents, probes, near_list, near_matrix):
    block_len = near_matrix.shape[2]
    blocks = near_list.shape[0]
    select = (near_list[:, :, None] == jnp.arange(blocks, dtype=jnp.int32)[None, None, :]).astype(F32)
    cur_blocks = currents.reshape(3, blocks, block_len)
    gathered = jnp.einsum("ctj,bnt->cbnj", cur_blocks, select, precision=lax.Precision.HIGHEST)
    g_hi, g_lo = split_outside(gathered)
    forward = jnp.einsum(
        "cbnj,bnij->cbi", jnp.concatenate([g_hi, g_lo]), near_matrix, preferred_element_type=F32
    )
    p_hi, p_lo = split_outside(probes.reshape(3, blocks, block_len))
    spread = jnp.einsum(
        "cbi,bnij->cbnj", jnp.concatenate([p_hi, p_lo]), near_matrix, preferred_element_type=F32
    )
    adjoint = jnp.einsum(
        "cbnj,bnt->ctj", spread[:3] + spread[3:], select, precision=lax.Precision.HIGHEST
    )
    return (forward[:3] + forward[3:]).reshape(3, -1), adjoint.reshape(3, -1)


def on_device(
    currents, probes, proj_weights, interp_weights, owner, cell, near_list, near_matrix, kernel_hat
):
    devices = lax.axis_size("row") * lax.axis_size("col")
    elem_count = currents.shape[1]
    capacity = 2 * elem_count // devices
    dz_count, ky_local, grid_x = kernel_hat.shape
    assert dz_count == 1
    grid_y = ky_local * devices
    x_local = grid_x // devices
    slots = devices * capacity
    n1 = grid_y // LANES
    per = ky_local // n1
    k1l = n1 // HALVES

    codes = x_local * grid_y
    assert codes & (codes - 1) == 0

    target = owner[:, 0]
    row, col = cell // grid_y % (x_local - 1), cell % grid_y
    key = target * codes + col * x_local + row
    columns = [*currents, *probes, *proj_weights, *interp_weights]
    order = lax.iota(jnp.int32, elem_count)
    key, *columns, order = lax.sort((key, *columns, order), num_keys=1, is_stable=False)
    bounds_of = jnp.arange(devices + 1, dtype=jnp.int32)
    starts = jnp.sum((target[None, :] < bounds_of[:, None]).astype(jnp.int32), axis=1)
    outgoing = expand_call(
        starts, key[None, :], [x[None, :] for x in columns], devices, capacity, codes
    )
    arrived = lax.all_to_all(outgoing, AXES, split_axis=0, concat_axis=0, tiled=True)
    payload, rc, bounds = gather_groups(arrived, x_local, CHUNK)

    yhi, ylo = split_np(y_table(devices, per))
    ty_cos, ty_sin = (jnp.asarray(t, F32) for t in phases(n1, LANES, grid_y))
    tx_cos, tx_sin = (
        jnp.asarray(np.tile(t, (1, k1l)), F32) for t in phases(devices, x_local, grid_x)
    )
    fwd, inv = split_np(x_table(x_local, -1.0)), split_np(x_table(x_local, 1.0))

    kernel_view = kernel_hat.reshape(per, HALVES, k1l, x_local, devices)
    kernel_t = jnp.transpose(kernel_view, (4, 1, 0, 2, 3)) * (1.0 / (grid_x * grid_y))
    kernel_t = kernel_t.reshape(devices * HALVES * per, k1l * x_local)

    def exchange(x):
        shaped = x.reshape(devices, 2 * HALVES * per, x.shape[1])
        moved = lax.all_to_all(shaped, AXES, split_axis=0, concat_axis=0, tiled=True)
        return moved.reshape(x.shape)

    def sample(products, *after):
        return sample_call(
            products, bounds, rc, payload, yhi, ylo, ty_cos, ty_sin, x_local, grid_y, after
        )

    def spectral(spectra, *after):
        return exchange(spectral_call(spectra, kernel_t, fwd, inv, tx_cos, tx_sin, devices, after))

    spectra, after = [], ()
    for field in range(3):
        grids = project_call(
            field, bounds, rc, payload, yhi, ylo, ty_cos, ty_sin, x_local, grid_y, after
        )
        spectra.append(exchange(grids))
        after = (grids,)
    products = [spectral(spectra[0]), spectral(spectra[1])]
    first = sample(products[0])
    products.append(spectral(spectra[2], first))
    second = sample(products[1])
    third = sample(products[2], second)
    results = [first, second, third]
    returning = scatter_groups(jnp.concatenate(results, axis=0), devices, capacity)
    returned = lax.all_to_all(returning, AXES, split_axis=0, concat_axis=0, tiled=True)
    homed = compact_call(starts, returned, elem_count)
    _, *homed = lax.sort((order, *homed), num_keys=1, is_stable=False)
    near_forward, near_adjoint = near_terms(currents, probes, near_list, near_matrix)
    return (jnp.stack(homed[0::2]) + near_forward, jnp.stack(homed[1::2]) + near_adjoint)


def solution(mesh):
    return jax.shard_map(
        on_device,
        mesh=mesh,
        in_specs=(
            P(None, AXES),
            P(None, AXES),
            P(None, AXES),
            P(None, AXES),
            P(AXES, None),
            P(AXES),
            P(AXES, None),
            P(AXES, None, None, None),
            P(None, AXES, None),
        ),
        out_specs=(P(None, AXES), P(None, AXES)),
        check_vma=False,
    )
```

```python
import math

import jax
import jax.numpy as jnp
import numpy as np
from jax import lax
from jax.experimental import pallas as pl
from jax.experimental.pallas import tpu as pltpu
from jax.sharding import PartitionSpec as P

AXES = ("row", "col")
LANES = 128
HALVES = 2
GROUP = 8
CHUNK = 1024
FIRST = 768
WINDOW = 256
F32 = jnp.float32
BF16 = jnp.bfloat16
NT = (((1,), (1,)), ((), ()))
NN = (((1,), (0,)), ((), ()))


def split_np(table):
    hi = table.astype(np.float32).astype(jnp.bfloat16)
    lo = (table - hi.astype(np.float64)).astype(np.float32).astype(jnp.bfloat16)
    return jnp.asarray(hi), jnp.asarray(lo)


def split(x):
    hi = x.astype(BF16)
    return hi, (x - hi.astype(F32)).astype(BF16)


def dot(a, b, dims):
    return lax.dot_general(a, b, dims, preferred_element_type=F32)


def dot3(a, b, dims):
    (ah, al), (bh, bl) = a, b
    return dot(ah, bh, dims) + (dot(ah, bl, dims) + dot(al, bh, dims))


def y_table(devices, per):
    d, c, h, q, hh, cc, y = np.ix_(
        range(devices), range(2), range(HALVES), range(per), range(HALVES), range(2), range(LANES)
    )
    angle = 2.0 * math.pi * (((d * per + q) * y) % LANES) / LANES
    sine = np.where(c < cc, 1.0, -1.0) * np.sin(angle)
    value = np.where(c == cc, np.cos(angle), sine) * (h == hh)
    return value.reshape(devices * 2 * HALVES * per, HALVES * 2 * LANES)


def x_table(length, direction):
    copies = LANES // length
    c, p, x, cc, pp, k = np.ix_(
        range(2), range(copies), range(length), range(2), range(copies), range(length)
    )
    angle = direction * 2.0 * math.pi * ((x * k) % length) / length
    sine = np.where(c < cc, 1.0, -1.0) * np.sin(angle)
    value = np.where(c == cc, np.cos(angle), sine) * (p == pp)
    return value.reshape(2 * LANES, 2 * LANES)


def phases(rows, cols, length):
    turns = (np.arange(rows)[:, None] * np.arange(cols)[None, :]) % length
    angle = 2.0 * math.pi * turns / length
    return np.cos(angle), np.sin(angle)


def fft_list(re, im, direction):
    n = len(re)
    if n == 1:
        return re, im
    even_re, even_im = fft_list(re[0::2], im[0::2], direction)
    odd_re, odd_im = fft_list(re[1::2], im[1::2], direction)
    low_re, low_im, high_re, high_im = [], [], [], []
    for k in range(n // 2):
        a, b = odd_re[k], odd_im[k]
        if k == 0:
            tr, ti = a, b
        elif 4 * k == n:
            tr, ti = (-b, a) if direction > 0 else (b, -a)
        else:
            cos = math.cos(2.0 * math.pi * k / n)
            sin = direction * math.sin(2.0 * math.pi * k / n)
            tr, ti = a * cos - b * sin, a * sin + b * cos
        low_re.append(even_re[k] + tr)
        low_im.append(even_im[k] + ti)
        high_re.append(even_re[k] - tr)
        high_im.append(even_im[k] - ti)
    return low_re + high_re, low_im + high_im


def one_hot(cols, start, size):
    ids = lax.broadcasted_iota(jnp.int32, (size, cols.shape[1]), 0) + start
    return jnp.where(ids == cols, 1.0, 0.0).astype(BF16)


def call(kernel, name, out_shape, args, scratch=(), smem_in=(), smem_out=(), far=(), flops=0, after=()):
    if after:
        count, inner = len(args), kernel
        kernel = lambda *refs: inner(*refs[:count], *refs[count + len(after) :])
    spaces = [
        pltpu.SMEM if i in smem_in else pl.ANY if i in far else pltpu.VMEM for i in range(len(args))
    ]
    outs = [pltpu.SMEM if i in smem_out else pltpu.VMEM for i in range(len(out_shape))]
    moved = sum(math.prod(x.shape) * x.dtype.itemsize for x in (*args, *out_shape))
    return pl.pallas_call(
        kernel,
        out_shape=list(out_shape),
        in_specs=[pl.BlockSpec(memory_space=space) for space in spaces]
        + [pl.BlockSpec(memory_space=pl.ANY)] * len(after),
        out_specs=[pl.BlockSpec(memory_space=space) for space in outs],
        scratch_shapes=list(scratch),
        compiler_params=pltpu.CompilerParams(vmem_limit_bytes=48 << 20),
        cost_estimate=pl.CostEstimate(flops=flops, transcendentals=0, bytes_accessed=moved),
        name=name,
    )(*args, *after)


def fetch(pairs, sems):
    copies = [pltpu.make_async_copy(src, dst, sems.at[i]) for i, (src, dst) in enumerate(pairs)]
    for copy in copies:
        copy.start()

    def wait():
        for copy in copies:
            copy.wait()

    return wait


def shape(dims, dtype=F32):
    return jax.ShapeDtypeStruct(dims, dtype)


def expand_call(starts, keys, rows, devices, capacity, codes):
    count = keys.shape[1]
    wide = -(-capacity // LANES) * LANES + LANES
    height = 16

    def kernel(starts_ref, key_ref, *refs):
        row_refs, out_ref, s_ref = refs[:-2], refs[-2], refs[-1]
        s_ref[:, count:] = jnp.zeros((height, wide), F32)
        for i, ref in enumerate(row_refs):
            s_ref[i : i + 1, 0:count] = ref[...]
        s_ref[height - 1 : height, 0:count] = (key_ref[...] & (codes - 1)).astype(F32)
        lane = lax.broadcasted_iota(jnp.int32, (height, wide), 1)
        rank = lax.broadcasted_iota(jnp.int32, (height, wide), 0)
        free = jnp.where(rank == height - 1, -1.0, 0.0)

        @pl.loop(0, devices)
        def _(d):
            first = starts_ref[d]
            held = starts_ref[d + 1] - first
            tile = first // LANES
            block = s_ref[:, pl.ds(pl.multiple_of(tile * LANES, LANES), wide)]
            moved = pltpu.roll(block, wide - (first - tile * LANES), 1)
            kept = jnp.where(lane < held, moved, free)
            out_ref[d] = jnp.where(rank == height - 2, held.astype(F32), kept)[:, :capacity]

    (out,) = call(
        kernel,
        "expand",
        [shape((devices, height, capacity))],
        [starts, keys, *rows],
        scratch=[pltpu.VMEM((height, count + wide), F32)],
        smem_in=(0,),
    )
    return out


def compact_call(starts, data, count):
    devices, height, capacity = data.shape
    wide = -(-capacity // LANES) * LANES + LANES

    def kernel(starts_ref, in_ref, out_ref, s_ref):
        lane = lax.broadcasted_iota(jnp.int32, (height, wide), 1)

        @pl.loop(0, devices)
        def _(d):
            first = starts_ref[d]
            held = starts_ref[d + 1] - first
            tile = first // LANES
            shift = first - tile * LANES
            at = pl.ds(pl.multiple_of(tile * LANES, LANES), wide)
            filler = jnp.zeros((height, wide - capacity), F32)
            moved = pltpu.roll(jnp.concatenate([in_ref[d], filler], axis=1), shift, 1)
            keep = (lane >= shift) & (lane < shift + held)
            s_ref[:, at] = jnp.where(keep, moved, s_ref[:, at])

        out_ref[...] = s_ref[:, :count]

    (out,) = call(
        kernel,
        "compact",
        [shape((height, count))],
        [starts, data],
        scratch=[pltpu.VMEM((height, count + wide), F32)],
        smem_in=(0,),
    )
    return out


def turn_blocks(parts):
    parts = list(parts)
    block = lax.broadcasted_iota(jnp.int32, parts[0].shape, 1) // GROUP
    for m in (1, 2, 4, 8):
        high = (block & m) != 0
        for i in range(16):
            if i & m == 0:
                a, b = parts[i], parts[i + m]
                parts[i] = jnp.where(high, pltpu.roll(b, m * GROUP, 1), a)
                parts[i + m] = jnp.where(high, b, pltpu.roll(a, LANES - m * GROUP, 1))
    return parts


def pick_lanes(tiles, place):
    dims = tiles[0].shape
    index = jnp.broadcast_to(jnp.clip(place, 0.0, len(tiles) * LANES - 1.0).astype(jnp.int32), dims)
    result = None
    for k, tile in enumerate(tiles):
        part = jnp.take_along_axis(tile, index & (LANES - 1), axis=1)
        result = part if k == 0 else jnp.where(index < k * LANES, result, part)
    return result


def gather_groups(arrived, x_local, chunk):
    devices, height, capacity = arrived.shape
    slots = devices * capacity
    chunks = slots // chunk
    shift = x_local.bit_length() - 1
    none = 1 << 20

    def decode(code):
        return code & (x_local - 1), lax.shift_right_arithmetic(code, shift)

    if capacity % LANES or devices % 16:
        turned = arrived.reshape(devices, height, capacity // GROUP, GROUP)
        turned = jnp.transpose(turned, (1, 2, 0, 3)).reshape(height, slots)
        row, col = decode(turned[height - 1].astype(jnp.int32))
        per_chunk = col.reshape(chunks, chunk)
        low = jnp.min(jnp.where(per_chunk < 0, none, per_chunk), axis=1)
        bounds = jnp.stack([low, jnp.max(per_chunk, axis=1)])
        return turned, jnp.stack([row, col]), bounds, jnp.zeros((8, LANES), F32)

    tiles = capacity // LANES

    def kernel(in_ref, out_ref, rc_ref, bound_ref, held_ref):
        most = jnp.zeros((1, LANES), F32)
        for i in range(devices):
            held = in_ref[i, height - 2 : height - 1, :LANES]
            held_ref[i : i + 1] = held
            most = jnp.maximum(most, held)
        held_ref[devices:] = jnp.broadcast_to(most, (8, LANES))
        per = 1.0 / jnp.maximum(most, 1.0)
        lane = lax.broadcasted_iota(jnp.int32, (1, LANES), 1).astype(F32)
        rank = lax.broadcasted_iota(jnp.int32, (height, LANES), 0)
        free = jnp.where(rank == height - 1, -1.0, 0.0)

        @pl.loop(0, devices // 16)
        def _(sb):
            for t in range(tiles):
                slot = lane + t * LANES
                parts = []
                for i in range(16):
                    sender = sb * 16 + i
                    held = in_ref[sender, height - 2 : height - 1, :LANES]
                    place = jnp.floor((slot * held + 0.5) * per)
                    before = jnp.floor(((slot - 1.0) * held + 0.5) * per)
                    valid = (place > before) & (slot < most)
                    picked = pick_lanes([in_ref[sender, :, k * LANES : (k + 1) * LANES] for k in range(tiles)], place)
                    parts.append(jnp.where(valid, picked, free))
                for j, part in enumerate(turn_blocks(parts)):
                    left = (t * 16 + j) * devices * GROUP
                    at = pl.ds(pl.multiple_of(left + sb * LANES, LANES), LANES)
                    out_ref[:, at] = part
                    row, col = decode(part[height - 1 :].astype(jnp.int32))
                    rc_ref[0:1, at] = row
                    rc_ref[1:2, at] = col

        @pl.loop(0, chunks)
        def _(i):
            col = rc_ref[1:2, pl.ds(pl.multiple_of(i * chunk, chunk), chunk)]
            bound_ref[0, i] = jnp.min(jnp.where(col < 0, none, col))
            bound_ref[1, i] = jnp.max(col)

    return call(
        kernel,
        "groups",
        [
            shape((height, slots)),
            shape((2, slots), jnp.int32),
            shape((2, chunks), jnp.int32),
            shape((devices + 8, LANES)),
        ],
        [arrived],
        smem_out=(2,),
    )


def scatter_groups(results, held, devices, capacity):
    height = results.shape[0]
    if capacity % LANES or devices % 16:
        turned = results.reshape(height, capacity // GROUP, devices, GROUP)
        return jnp.transpose(turned, (2, 0, 1, 3)).reshape(devices, height, capacity)

    tiles = capacity // LANES

    def kernel(in_ref, held_ref, out_ref):
        most = held_ref[devices : devices + 1]
        lane = lax.broadcasted_iota(jnp.int32, (1, LANES), 1).astype(F32)

        @pl.loop(0, devices // 16)
        def _(sb):
            turned = []
            for t in range(tiles):
                parts = []
                for j in range(16):
                    left = (t * 16 + j) * devices * GROUP
                    parts.append(in_ref[:, pl.ds(pl.multiple_of(left + sb * LANES, LANES), LANES)])
                turned.append(turn_blocks(parts))
            for i in range(16):
                sender = sb * 16 + i
                here = jnp.maximum(held_ref[pl.ds(sender, 1)], 1.0)
                for t in range(tiles):
                    place = jnp.floor(((lane + t * LANES) * most + here - 0.5) / here)
                    picked = pick_lanes([turned[k][i] for k in range(tiles)], place)
                    out_ref[sender, :, t * LANES : (t + 1) * LANES] = picked

    (out,) = call(kernel, "ungroup", [shape((devices, height, capacity))], [results, held])
    return out


def visit_windows(bound_ref, i, visit):
    first = bound_ref[0, i] // LANES * LANES
    visit(pl.multiple_of(first, LANES), FIRST, True)
    start = first + FIRST
    more = (bound_ref[1, i] - start) // WINDOW + 1

    def step(w, carry):
        visit(pl.multiple_of(start + w * WINDOW, LANES), WINDOW, False)
        return carry

    lax.fori_loop(0, more, step, 0)


def project_call(field, bounds, rc, payload, yhi, ylo, tw_cos, tw_sin, x_local, grid_y):
    slots = rc.shape[1]
    chunks = bounds.shape[1]
    chunk = slots // chunks
    n1 = grid_y // LANES
    k1l = n1 // HALVES
    rows = k1l * x_local
    width = HALVES * 2 * LANES
    half = 4 * x_local

    def kernel(bound_ref, rc_ref, pay_ref, yhi_ref, ylo_ref, cos_ref, sin_ref, out_ref, v_ref, acc_ref, g_ref, x_ref, hi_ref, lo_ref, sems):
        tables_here = fetch([(yhi_ref, hi_ref), (ylo_ref, lo_ref)], sems)
        acc_ref[...] = jnp.zeros(acc_ref.shape, F32)

        @pl.loop(0, chunks)
        def _(i):
            @pl.when(bound_ref[1, i] >= 0)
            def _():
                at = pl.ds(pl.multiple_of(i * chunk, chunk), chunk)
                ids = lax.broadcasted_iota(jnp.int32, (x_local, chunk), 0)
                m0 = ids == rc_ref[0:1, at]
                m1 = ids == rc_ref[0:1, at] + 1
                for c in range(2):
                    u = pay_ref[3 * c + field : 3 * c + field + 1, at]
                    for b in range(2):
                        p0 = u * pay_ref[6 + 4 * c + b : 7 + 4 * c + b, at]
                        p1 = u * pay_ref[8 + 4 * c + b : 9 + 4 * c + b, at]
                        hi, lo = split(jnp.where(m0, p0, jnp.where(m1, p1, 0.0)))
                        base = (b * 2 + c) * x_local
                        v_ref[base : base + x_local, :] = hi
                        v_ref[half + base : half + base + x_local, :] = lo

                def visit(start, size, fresh):
                    to = pl.ds(start, size)
                    acc_ref[:, to] += dot(v_ref[...], one_hot(rc_ref[1:2, at], start, size), NT)

                visit_windows(bound_ref, i, visit)

        total = acc_ref[:half, :grid_y] + acc_ref[half:, :grid_y]
        g_ref[...] = total[: 2 * x_local] + pltpu.roll(total[2 * x_local :], 1, 1)

        @pl.loop(0, x_local // 8)
        def _(i):
            re_at = pl.ds(pl.multiple_of(i * 8, 8), 8)
            im_at = pl.ds(pl.multiple_of(x_local + i * 8, 8), 8)
            re = [g_ref[re_at, y * LANES : (y + 1) * LANES] for y in range(n1)]
            im = [g_ref[im_at, y * LANES : (y + 1) * LANES] for y in range(n1)]
            re, im = fft_list(re, im, -1.0)
            for k in range(n1):
                cos, sin = cos_ref[k : k + 1, :], sin_ref[k : k + 1, :]
                to = pl.ds(pl.multiple_of((k % k1l) * x_local + i * 8, 8), 8)
                left = (k // k1l) * 2 * LANES
                x_ref[to, left : left + LANES] = re[k] * cos + im[k] * sin
                x_ref[to, left + LANES : left + 2 * LANES] = im[k] * cos - re[k] * sin

        tables_here()
        out_ref[...] = dot3((hi_ref[...], lo_ref[...]), split(x_ref[...]), NT)

    (out,) = call(
        kernel,
        "project",
        [shape((yhi.shape[0], rows))],
        [bounds, rc, payload, yhi, ylo, tw_cos, tw_sin],
        scratch=[
            pltpu.VMEM((2 * half, chunk), BF16),
            pltpu.VMEM((2 * half, grid_y + FIRST), F32),
            pltpu.VMEM((2 * x_local, grid_y), F32),
            pltpu.VMEM((rows, width), F32),
            pltpu.VMEM(yhi.shape, BF16),
            pltpu.VMEM(ylo.shape, BF16),
            pltpu.SemaphoreType.DMA((2,)),
        ],
        smem_in=(0,),
        far=(3, 4),
        flops=4 * half * slots * grid_y,
    )
    return out


def spectral_call(data, kernel_t, fwd, inv, tw_cos, tw_sin, devices, after):
    lanes = data.shape[1]
    rows = data.shape[0] // (2 * devices)

    def kernel(in_ref, kt_ref, fh_ref, fl_ref, ih_ref, il_ref, cos_ref, sin_ref, out_ref, re_ref, im_ref):
        @pl.loop(0, lanes // LANES)
        def _(t):
            at = pl.ds(pl.multiple_of(t * LANES, LANES), LANES)
            re = [in_ref[(2 * s) * rows : (2 * s + 1) * rows, at] for s in range(devices)]
            im = [in_ref[(2 * s + 1) * rows : (2 * s + 2) * rows, at] for s in range(devices)]
            re, im = fft_list(re, im, -1.0)
            for k in range(devices):
                cos, sin = cos_ref[k : k + 1, at], sin_ref[k : k + 1, at]
                re_ref[k * rows : (k + 1) * rows, at] = re[k] * cos + im[k] * sin
                im_ref[k * rows : (k + 1) * rows, at] = im[k] * cos - re[k] * sin

        for t in range(lanes // LANES):
            at = slice(t * LANES, (t + 1) * LANES)
            both = jnp.concatenate([re_ref[:, at], im_ref[:, at]], axis=1)
            spectrum = dot3(split(both), (fh_ref[...], fl_ref[...]), NN)
            factor = kt_ref[:, at]
            both = jnp.concatenate([spectrum[:, :LANES] * factor, spectrum[:, LANES:] * factor], axis=1)
            back = dot3(split(both), (ih_ref[...], il_ref[...]), NN)
            re_ref[:, at] = back[:, :LANES]
            im_ref[:, at] = back[:, LANES:]

        @pl.loop(0, lanes // LANES)
        def _(t):
            at = pl.ds(pl.multiple_of(t * LANES, LANES), LANES)
            re, im = [], []
            for k in range(devices):
                cos, sin = cos_ref[k : k + 1, at], sin_ref[k : k + 1, at]
                a = re_ref[k * rows : (k + 1) * rows, at]
                b = im_ref[k * rows : (k + 1) * rows, at]
                re.append(a * cos - b * sin)
                im.append(b * cos + a * sin)
            re, im = fft_list(re, im, 1.0)
            for s in range(devices):
                out_ref[(2 * s) * rows : (2 * s + 1) * rows, at] = re[s]
                out_ref[(2 * s + 1) * rows : (2 * s + 2) * rows, at] = im[s]

    (out,) = call(
        kernel,
        "spectral",
        [shape(data.shape)],
        [data, kernel_t, *fwd, *inv, tw_cos, tw_sin],
        scratch=[
            pltpu.VMEM((devices * rows, lanes), F32),
            pltpu.VMEM((devices * rows, lanes), F32),
        ],
        flops=1 << 30,
        after=after,
    )
    return out


def sample_call(data, bounds, rc, payload, yhi, ylo, tw_cos, tw_sin, x_local, grid_y, after):
    slots = rc.shape[1]
    n1 = grid_y // LANES
    k1l = n1 // HALVES
    rows = k1l * x_local
    width = HALVES * 2 * LANES
    chunks = bounds.shape[1]
    chunk = slots // chunks
    half = 4 * x_local

    def kernel(in_ref, bound_ref, rc_ref, pay_ref, yhi_ref, ylo_ref, cos_ref, sin_ref, out_ref, u_ref, g_ref, p_ref, t_ref, hi_ref, lo_ref, sems):
        tables_here = fetch([(yhi_ref, hi_ref), (ylo_ref, lo_ref)], sems)
        turned = split(jnp.transpose(in_ref[...]))
        tables_here()
        u_ref[...] = dot3(turned, (hi_ref[...], lo_ref[...]), NN)

        @pl.loop(0, x_local // 8)
        def _(i):
            re, im = [], []
            for k in range(n1):
                cos, sin = cos_ref[k : k + 1, :], sin_ref[k : k + 1, :]
                at = pl.ds(pl.multiple_of((k % k1l) * x_local + i * 8, 8), 8)
                left = (k // k1l) * 2 * LANES
                a = u_ref[at, left : left + LANES]
                b = u_ref[at, left + LANES : left + 2 * LANES]
                re.append(a * cos - b * sin)
                im.append(b * cos + a * sin)
            re, im = fft_list(re, im, 1.0)
            re_at = pl.ds(pl.multiple_of(i * 8, 8), 8)
            im_at = pl.ds(pl.multiple_of(x_local + i * 8, 8), 8)
            for y in range(n1):
                g_ref[re_at, y * LANES : (y + 1) * LANES] = re[y]
                g_ref[im_at, y * LANES : (y + 1) * LANES] = im[y]

        hi, lo = split(g_ref[...])
        p_ref[0 : 2 * x_local, :grid_y] = hi
        p_ref[half : half + 2 * x_local, :grid_y] = lo
        hi, lo = split(pltpu.roll(g_ref[...], grid_y - 1, 1))
        p_ref[2 * x_local : half, :grid_y] = hi
        p_ref[half + 2 * x_local :, :grid_y] = lo
        p_ref[:, grid_y:] = jnp.zeros((2 * half, FIRST), BF16)

        out_ref[...] = jnp.zeros(out_ref.shape, F32)

        @pl.loop(0, chunks)
        def _(i):
            @pl.when(bound_ref[1, i] >= 0)
            def _():
                at = pl.ds(pl.multiple_of(i * chunk, chunk), chunk)

                def visit(start, size, fresh):
                    of = pl.ds(start, size)
                    part = dot(p_ref[:, of], one_hot(rc_ref[1:2, at], start, size), NN)
                    t_ref[...] = part if fresh else t_ref[...] + part

                visit_windows(bound_ref, i, visit)
                total = t_ref[:half] + t_ref[half:]
                ids = lax.broadcasted_iota(jnp.int32, (x_local, chunk), 0)
                m0 = ids == rc_ref[0:1, at]
                m1 = ids == rc_ref[0:1, at] + 1
                for c in range(2):
                    result = jnp.zeros((x_local, chunk), F32)
                    for b in range(2):
                        other = 10 - 4 * c
                        w0 = pay_ref[other + b : other + b + 1, at]
                        w1 = pay_ref[other + 2 + b : other + 3 + b, at]
                        base = (b * 2 + c) * x_local
                        weight = jnp.where(m0, w0, jnp.where(m1, w1, 0.0))
                        result = result + weight * total[base : base + x_local]
                    out_ref[c : c + 1, at] = jnp.sum(result, axis=0, keepdims=True)

    (out,) = call(
        kernel,
        "sample",
        [shape((2, slots))],
        [data, bounds, rc, payload, yhi, ylo, tw_cos, tw_sin],
        scratch=[
            pltpu.VMEM((rows, width), F32),
            pltpu.VMEM((2 * x_local, grid_y), F32),
            pltpu.VMEM((2 * half, grid_y + FIRST), BF16),
            pltpu.VMEM((2 * half, chunk), F32),
            pltpu.VMEM(yhi.shape, BF16),
            pltpu.VMEM(ylo.shape, BF16),
            pltpu.SemaphoreType.DMA((2,)),
        ],
        smem_in=(1,),
        far=(4, 5),
        flops=4 * half * slots * grid_y,
        after=after,
    )
    return out


def split_outside(x):
    hi = lax.reduce_precision(x, 8, 7)
    return hi.astype(BF16), (x - hi).astype(BF16)


def near_terms(currents, probes, near_list, near_matrix):
    block_len = near_matrix.shape[2]
    blocks = near_list.shape[0]
    select = (near_list[:, :, None] == jnp.arange(blocks, dtype=jnp.int32)[None, None, :]).astype(F32)
    cur_blocks = currents.reshape(3, blocks, block_len)
    gathered = jnp.einsum("ctj,bnt->cbnj", cur_blocks, select, precision=lax.Precision.HIGHEST)
    g_hi, g_lo = split_outside(gathered)
    forward = jnp.einsum(
        "cbnj,bnij->cbi", jnp.concatenate([g_hi, g_lo]), near_matrix, preferred_element_type=F32
    )
    p_hi, p_lo = split_outside(probes.reshape(3, blocks, block_len))
    spread = jnp.einsum(
        "cbi,bnij->cbnj", jnp.concatenate([p_hi, p_lo]), near_matrix, preferred_element_type=F32
    )
    adjoint = jnp.einsum(
        "cbnj,bnt->ctj", spread[:3] + spread[3:], select, precision=lax.Precision.HIGHEST
    )
    return (forward[:3] + forward[3:]).reshape(3, -1), adjoint.reshape(3, -1)


def on_device(
    currents, probes, proj_weights, interp_weights, owner, cell, near_list, near_matrix, kernel_hat
):
    devices = lax.axis_size("row") * lax.axis_size("col")
    elem_count = currents.shape[1]
    capacity = 2 * elem_count // devices
    dz_count, ky_local, grid_x = kernel_hat.shape
    assert dz_count == 1
    grid_y = ky_local * devices
    x_local = grid_x // devices
    slots = devices * capacity
    n1 = grid_y // LANES
    per = ky_local // n1
    k1l = n1 // HALVES

    codes = x_local * grid_y
    assert codes & (codes - 1) == 0

    target = owner[:, 0]
    row, col = cell // grid_y % (x_local - 1), cell % grid_y
    key = target * codes + col * x_local + row
    columns = [*currents, *probes, *proj_weights, *interp_weights]
    order = lax.iota(jnp.int32, elem_count)
    key, *columns, order = lax.sort((key, *columns, order), num_keys=1, is_stable=False)
    bounds_of = jnp.arange(devices + 1, dtype=jnp.int32)
    starts = jnp.sum((target[None, :] < bounds_of[:, None]).astype(jnp.int32), axis=1)
    outgoing = expand_call(
        starts, key[None, :], [x[None, :] for x in columns], devices, capacity, codes
    )
    arrived = lax.all_to_all(outgoing, AXES, split_axis=0, concat_axis=0, tiled=True)
    payload, rc, bounds, held = gather_groups(arrived, x_local, CHUNK)

    yhi, ylo = split_np(y_table(devices, per))
    ty_cos, ty_sin = (jnp.asarray(t, F32) for t in phases(n1, LANES, grid_y))
    tx_cos, tx_sin = (
        jnp.asarray(np.tile(t, (1, k1l)), F32) for t in phases(devices, x_local, grid_x)
    )
    fwd, inv = split_np(x_table(x_local, -1.0)), split_np(x_table(x_local, 1.0))

    kernel_view = kernel_hat.reshape(per, HALVES, k1l, x_local, devices)
    kernel_t = jnp.transpose(kernel_view, (4, 1, 0, 2, 3)) * (1.0 / (grid_x * grid_y))
    kernel_t = kernel_t.reshape(devices * HALVES * per, k1l * x_local)

    def exchange(*fields):
        shaped = [x.reshape(devices, -1, x.shape[1]) for x in fields]
        height = shaped[0].shape[1]
        moved = lax.all_to_all(
            jnp.concatenate(shaped, axis=1), AXES, split_axis=0, concat_axis=0, tiled=True
        )
        parts = [moved[:, i * height : (i + 1) * height] for i in range(len(fields))]
        return [x.reshape(fields[0].shape) for x in parts]

    def spectral(spectra, *after):
        return spectral_call(spectra, kernel_t, fwd, inv, tx_cos, tx_sin, devices, after)

    def sample(products, *after):
        return sample_call(
            products, bounds, rc, payload, yhi, ylo, ty_cos, ty_sin, x_local, grid_y, after
        )

    spectra = []
    for field in range(3):
        grids = project_call(field, bounds, rc, payload, yhi, ylo, ty_cos, ty_sin, x_local, grid_y)
        spectra.extend(exchange(grids))
    products = exchange(spectral(spectra[0]), spectral(spectra[1]))
    products += exchange(spectral(spectra[2]))
    first = sample(products[0])
    second = sample(products[1])
    third = sample(products[2], first, second)
    results = [first, second, third]
    returning = scatter_groups(jnp.concatenate(results, axis=0), held, devices, capacity)
    returned = lax.all_to_all(returning, AXES, split_axis=0, concat_axis=0, tiled=True)
    homed = compact_call(starts, returned, elem_count)
    _, *homed = lax.sort((order, *homed), num_keys=1, is_stable=False)
    near_forward, near_adjoint = near_terms(currents, probes, near_list, near_matrix)
    return (jnp.stack(homed[0::2]) + near_forward, jnp.stack(homed[1::2]) + near_adjoint)


def solution(mesh):
    return jax.shard_map(
        on_device,
        mesh=mesh,
        in_specs=(
            P(None, AXES),
            P(None, AXES),
            P(None, AXES),
            P(None, AXES),
            P(AXES, None),
            P(AXES),
            P(AXES, None),
            P(AXES, None, None, None),
            P(None, AXES, None),
        ),
        out_specs=(P(None, AXES), P(None, AXES)),
        check_vma=False,
    )
```

```python
import math

import jax
import jax.numpy as jnp
import numpy as np
from jax import lax
from jax.experimental import pallas as pl
from jax.experimental.pallas import tpu as pltpu
from jax.sharding import PartitionSpec as P

AXES = ("row", "col")
LANES = 128
HALVES = 2
GROUP = 8
CHUNK = 1024
FIRST = 768
WINDOW = 256
F32 = jnp.float32
BF16 = jnp.bfloat16
NT = (((1,), (1,)), ((), ()))
NN = (((1,), (0,)), ((), ()))


def split_np(table):
    hi = table.astype(np.float32).astype(jnp.bfloat16)
    lo = (table - hi.astype(np.float64)).astype(np.float32).astype(jnp.bfloat16)
    return jnp.asarray(hi), jnp.asarray(lo)


def split(x):
    hi = x.astype(BF16)
    return hi, (x - hi.astype(F32)).astype(BF16)


def dot(a, b, dims):
    return lax.dot_general(a, b, dims, preferred_element_type=F32)


def dot3(a, b, dims):
    (ah, al), (bh, bl) = a, b
    return dot(ah, bh, dims) + (dot(ah, bl, dims) + dot(al, bh, dims))


def y_table(devices, per):
    d, c, h, q, hh, cc, y = np.ix_(
        range(devices), range(2), range(HALVES), range(per), range(HALVES), range(2), range(LANES)
    )
    angle = 2.0 * math.pi * (((d * per + q) * y) % LANES) / LANES
    sine = np.where(c < cc, 1.0, -1.0) * np.sin(angle)
    value = np.where(c == cc, np.cos(angle), sine) * (h == hh)
    return value.reshape(devices * 2 * HALVES * per, HALVES * 2 * LANES)


def x_table(length, direction):
    copies = LANES // length
    c, p, x, cc, pp, k = np.ix_(
        range(2), range(copies), range(length), range(2), range(copies), range(length)
    )
    angle = direction * 2.0 * math.pi * ((x * k) % length) / length
    sine = np.where(c < cc, 1.0, -1.0) * np.sin(angle)
    value = np.where(c == cc, np.cos(angle), sine) * (p == pp)
    return value.reshape(2 * LANES, 2 * LANES)


def phases(rows, cols, length):
    turns = (np.arange(rows)[:, None] * np.arange(cols)[None, :]) % length
    angle = 2.0 * math.pi * turns / length
    return np.cos(angle), np.sin(angle)


def fft_list(re, im, direction):
    n = len(re)
    if n == 1:
        return re, im
    even_re, even_im = fft_list(re[0::2], im[0::2], direction)
    odd_re, odd_im = fft_list(re[1::2], im[1::2], direction)
    low_re, low_im, high_re, high_im = [], [], [], []
    for k in range(n // 2):
        a, b = odd_re[k], odd_im[k]
        if k == 0:
            tr, ti = a, b
        elif 4 * k == n:
            tr, ti = (-b, a) if direction > 0 else (b, -a)
        else:
            cos = math.cos(2.0 * math.pi * k / n)
            sin = direction * math.sin(2.0 * math.pi * k / n)
            tr, ti = a * cos - b * sin, a * sin + b * cos
        low_re.append(even_re[k] + tr)
        low_im.append(even_im[k] + ti)
        high_re.append(even_re[k] - tr)
        high_im.append(even_im[k] - ti)
    return low_re + high_re, low_im + high_im


def one_hot(cols, start, size):
    ids = lax.broadcasted_iota(jnp.int32, (size, cols.shape[1]), 0) + start
    return jnp.where(ids == cols, 1.0, 0.0).astype(BF16)


def call(kernel, name, out_shape, args, scratch=(), smem_in=(), smem_out=(), far=(), flops=0, after=()):
    count, skip, results = len(args), len(after), len(out_shape)
    spaces = [
        pltpu.SMEM if i in smem_in else pl.ANY if i in far else pltpu.VMEM for i in range(count)
    ]
    outs = [pltpu.SMEM if i in smem_out else pltpu.VMEM for i in range(results)]
    moved = sum(math.prod(x.shape) * x.dtype.itemsize for x in (*args, *out_shape))
    near_by = [pltpu.VMEM(args[i].shape, args[i].dtype) for i in far]
    sems = [pltpu.SemaphoreType.DMA((len(far),))] if far else []

    def body(*refs):
        refs = refs[:count] + refs[count + skip :]
        if not far:
            return kernel(*refs)
        refs, targets, sem = list(refs[: -len(far) - 1]), refs[-len(far) - 1 : -1], refs[-1]
        copies = {}
        for j, i in enumerate(far):
            copies[i] = pltpu.make_async_copy(refs[i], targets[j], sem.at[j])
            copies[i].start()
            refs[i] = targets[j]

        def wait(*numbers):
            for i in numbers:
                copies[i].wait()

        return kernel(wait, *refs)

    return pl.pallas_call(
        body,
        out_shape=list(out_shape),
        in_specs=[pl.BlockSpec(memory_space=space) for space in spaces]
        + [pl.BlockSpec(memory_space=pl.ANY)] * skip,
        out_specs=[pl.BlockSpec(memory_space=space) for space in outs],
        scratch_shapes=[*scratch, *near_by, *sems],
        compiler_params=pltpu.CompilerParams(vmem_limit_bytes=32 << 20),
        cost_estimate=pl.CostEstimate(flops=flops, transcendentals=0, bytes_accessed=moved),
        name=name,
    )(*args, *after)


def shape(dims, dtype=F32):
    return jax.ShapeDtypeStruct(dims, dtype)


def expand_call(starts, keys, rows, devices, capacity, codes):
    count = keys.shape[1]
    wide = -(-capacity // LANES) * LANES + LANES
    height = 16

    def kernel(starts_ref, key_ref, *refs):
        row_refs, out_ref, s_ref = refs[:-2], refs[-2], refs[-1]
        s_ref[:, count:] = jnp.zeros((height, wide), F32)
        for i, ref in enumerate(row_refs):
            s_ref[i : i + 1, 0:count] = ref[...]
        s_ref[height - 1 : height, 0:count] = (key_ref[...] & (codes - 1)).astype(F32)
        lane = lax.broadcasted_iota(jnp.int32, (height, wide), 1)
        rank = lax.broadcasted_iota(jnp.int32, (height, wide), 0)
        free = jnp.where(rank == height - 1, -1.0, 0.0)

        @pl.loop(0, devices, unroll=4)
        def _(d):
            first = starts_ref[d]
            held = starts_ref[d + 1] - first
            tile = first // LANES
            block = s_ref[:, pl.ds(pl.multiple_of(tile * LANES, LANES), wide)]
            moved = pltpu.roll(block, wide - (first - tile * LANES), 1)
            kept = jnp.where(lane < held, moved, free)
            out_ref[d] = jnp.where(rank == height - 2, held.astype(F32), kept)[:, :capacity]

    (out,) = call(
        kernel,
        "expand",
        [shape((devices, height, capacity))],
        [starts, keys, *rows],
        scratch=[pltpu.VMEM((height, count + wide), F32)],
        smem_in=(0,),
    )
    return out


def compact_call(starts, data, count):
    devices, height, capacity = data.shape
    wide = -(-capacity // LANES) * LANES + LANES

    def kernel(starts_ref, in_ref, out_ref, s_ref, r_ref):
        lane = lax.broadcasted_iota(jnp.int32, (height, wide), 1)
        filler = jnp.zeros((height, wide - capacity), F32)

        @pl.loop(0, devices, unroll=4)
        def _(d):
            whole = jnp.concatenate([in_ref[d], filler], axis=1)
            r_ref[d] = pltpu.roll(whole, starts_ref[d] % LANES, 1)

        @pl.loop(0, devices)
        def _(d):
            first = starts_ref[d]
            shift = first % LANES
            left = pl.multiple_of(first - shift, LANES)
            edge = jnp.where(lane[:, :LANES] < shift, s_ref[:, pl.ds(left, LANES)], r_ref[d, :, :LANES])
            s_ref[:, pl.ds(left, LANES)] = edge
            s_ref[:, pl.ds(left + LANES, wide - LANES)] = r_ref[d, :, LANES:]

        out_ref[...] = s_ref[:, :count]

    (out,) = call(
        kernel,
        "compact",
        [shape((height, count))],
        [starts, data],
        scratch=[
            pltpu.VMEM((height, count + wide), F32),
            pltpu.VMEM((devices, height, wide), F32),
        ],
        smem_in=(0,),
    )
    return out


def turn_blocks(parts):
    parts = list(parts)
    block = lax.broadcasted_iota(jnp.int32, parts[0].shape, 1) // GROUP
    for m in (1, 2, 4, 8):
        high = (block & m) != 0
        for i in range(16):
            if i & m == 0:
                a, b = parts[i], parts[i + m]
                parts[i] = jnp.where(high, pltpu.roll(b, m * GROUP, 1), a)
                parts[i + m] = jnp.where(high, b, pltpu.roll(a, LANES - m * GROUP, 1))
    return parts


def pick_lanes(tiles, place):
    dims = tiles[0].shape
    index = jnp.broadcast_to(jnp.clip(place, 0.0, len(tiles) * LANES - 1.0).astype(jnp.int32), dims)
    result = None
    for k, tile in enumerate(tiles):
        part = jnp.take_along_axis(tile, index & (LANES - 1), axis=1)
        result = part if k == 0 else jnp.where(index < k * LANES, result, part)
    return result


def gather_groups(arrived, x_local, chunk):
    devices, height, capacity = arrived.shape
    slots = devices * capacity
    chunks = slots // chunk
    shift = x_local.bit_length() - 1
    none = 1 << 20

    def decode(code):
        return code & (x_local - 1), lax.shift_right_arithmetic(code, shift)

    if capacity % LANES or devices % 16:
        turned = arrived.reshape(devices, height, capacity // GROUP, GROUP)
        turned = jnp.transpose(turned, (1, 2, 0, 3)).reshape(height, slots)
        row, col = decode(turned[height - 1].astype(jnp.int32))
        per_chunk = col.reshape(chunks, chunk)
        low = jnp.min(jnp.where(per_chunk < 0, none, per_chunk), axis=1)
        bounds = jnp.stack([low, jnp.max(per_chunk, axis=1)])
        return turned, jnp.stack([row, col]), bounds, jnp.zeros((8, LANES), F32)

    tiles = capacity // LANES

    def kernel(in_ref, out_ref, rc_ref, bound_ref, held_ref):
        most = jnp.zeros((1, LANES), F32)
        for i in range(devices):
            held = in_ref[i, height - 2 : height - 1, :LANES]
            held_ref[i : i + 1] = held
            most = jnp.maximum(most, held)
        held_ref[devices:] = jnp.broadcast_to(most, (8, LANES))
        per = 1.0 / jnp.maximum(most, 1.0)
        lane = lax.broadcasted_iota(jnp.int32, (1, LANES), 1).astype(F32)
        rank = lax.broadcasted_iota(jnp.int32, (height, LANES), 0)
        free = jnp.where(rank == height - 1, -1.0, 0.0)

        @pl.loop(0, devices // 16 * tiles)
        def _(n):
            sb, t = n // tiles, n % tiles
            slot = lane + (t * LANES).astype(F32)
            parts = []
            for i in range(16):
                sender = sb * 16 + i
                held = in_ref[sender, height - 2 : height - 1, :LANES]
                place = jnp.floor((slot * held + 0.5) * per)
                before = jnp.floor(((slot - 1.0) * held + 0.5) * per)
                valid = (place > before) & (slot < most)
                across = [in_ref[sender, :, k * LANES : (k + 1) * LANES] for k in range(tiles)]
                parts.append(jnp.where(valid, pick_lanes(across, place), free))
            for j, part in enumerate(turn_blocks(parts)):
                left = (t * 16 + j) * devices * GROUP + sb * LANES
                at = pl.ds(pl.multiple_of(left, LANES), LANES)
                out_ref[:, at] = part
                row, col = decode(part[height - 1 :].astype(jnp.int32))
                rc_ref[0:1, at] = row
                rc_ref[1:2, at] = col

        @pl.loop(0, chunks)
        def _(i):
            col = rc_ref[1:2, pl.ds(pl.multiple_of(i * chunk, chunk), chunk)]
            bound_ref[0, i] = jnp.min(jnp.where(col < 0, none, col))
            bound_ref[1, i] = jnp.max(col)

    return call(
        kernel,
        "groups",
        [
            shape((height, slots)),
            shape((2, slots), jnp.int32),
            shape((2, chunks), jnp.int32),
            shape((devices + 8, LANES)),
        ],
        [arrived],
        smem_out=(2,),
    )


def scatter_groups(results, held, devices, capacity):
    height = results.shape[0]
    if capacity % LANES or devices % 16:
        turned = results.reshape(height, capacity // GROUP, devices, GROUP)
        return jnp.transpose(turned, (2, 0, 1, 3)).reshape(devices, height, capacity)

    tiles = capacity // LANES

    def kernel(in_ref, held_ref, out_ref):
        most = held_ref[devices : devices + 1]
        lane = lax.broadcasted_iota(jnp.int32, (1, LANES), 1).astype(F32)

        @pl.loop(0, devices // 16)
        def _(sb):
            turned = []
            for t in range(tiles):
                parts = []
                for j in range(16):
                    left = (t * 16 + j) * devices * GROUP
                    parts.append(in_ref[:, pl.ds(pl.multiple_of(left + sb * LANES, LANES), LANES)])
                turned.append(turn_blocks(parts))
            for i in range(16):
                sender = sb * 16 + i
                here = jnp.maximum(held_ref[pl.ds(sender, 1)], 1.0)
                for t in range(tiles):
                    place = jnp.floor(((lane + t * LANES) * most + here - 0.5) / here)
                    picked = pick_lanes([turned[k][i] for k in range(tiles)], place)
                    out_ref[sender, :, t * LANES : (t + 1) * LANES] = picked

    (out,) = call(kernel, "ungroup", [shape((devices, height, capacity))], [results, held])
    return out


def visit_windows(bound_ref, i, visit):
    first = pl.multiple_of(bound_ref[0, i] // LANES * LANES, LANES)
    visit(first, FIRST)

    def step(w, carry):
        visit(pl.multiple_of(first + FIRST + w * WINDOW, LANES), WINDOW)
        return carry

    lax.fori_loop(0, (bound_ref[1, i] - first - FIRST) // WINDOW + 1, step, 0)


def project_call(field, bounds, rc, payload, table, tw_cos, tw_sin, x_local, grid_y):
    slots = rc.shape[1]
    chunks = bounds.shape[1]
    chunk = slots // chunks
    n1 = grid_y // LANES
    k1l = n1 // HALVES
    rows = k1l * x_local
    width = HALVES * 2 * LANES
    half = 4 * x_local

    def kernel(wait, bound_ref, rc_ref, pay_ref, table_ref, cos_ref, sin_ref, out_ref, v_ref, acc_ref, x_ref):
        @pl.loop(0, half // 32)
        def _(i):
            acc_ref[pl.ds(pl.multiple_of(i * 64, 64), 64)] = jnp.zeros((64, acc_ref.shape[1]), F32)

        wait(1, 2)

        @pl.loop(0, chunks)
        def _(i):
            @pl.when(bound_ref[1, i] >= 0)
            def _():
                @pl.loop(0, chunk // 256)
                def _(j):
                    at = pl.ds(pl.multiple_of(i * chunk + j * 256, 256), 256)
                    to = pl.ds(pl.multiple_of(j * 256, 256), 256)
                    ids = lax.broadcasted_iota(jnp.int32, (x_local, 256), 0)
                    m0 = ids == rc_ref[0:1, at]
                    m1 = ids == rc_ref[0:1, at] + 1
                    for c in range(2):
                        u = pay_ref[3 * c + field : 3 * c + field + 1, at]
                        for b in range(2):
                            p0 = u * pay_ref[6 + 4 * c + b : 7 + 4 * c + b, at]
                            p1 = u * pay_ref[8 + 4 * c + b : 9 + 4 * c + b, at]
                            hi, lo = split(jnp.where(m0, p0, jnp.where(m1, p1, 0.0)))
                            base = (b * 2 + c) * x_local
                            v_ref[base : base + x_local, to] = hi
                            v_ref[half + base : half + base + x_local, to] = lo

                col = rc_ref[1:2, pl.ds(pl.multiple_of(i * chunk, chunk), chunk)]

                def visit(start, size):
                    acc_ref[:, pl.ds(start, size)] += dot(v_ref[...], one_hot(col, start, size), NT)

                visit_windows(bound_ref, i, visit)

        wait(3, 4, 5)

        @pl.loop(0, x_local // 8)
        def _(i):
            def rows_of(base):
                low = pl.ds(pl.multiple_of(base + i * 8, 8), 8)
                high = pl.ds(pl.multiple_of(half + base + i * 8, 8), 8)
                return acc_ref[low, :grid_y] + acc_ref[high, :grid_y]

            parts = []
            for c in range(2):
                g = rows_of(c * x_local) + pltpu.roll(rows_of((2 + c) * x_local), 1, 1)
                parts.append([g[:, y * LANES : (y + 1) * LANES] for y in range(n1)])
            re, im = fft_list(parts[0], parts[1], -1.0)
            for k in range(n1):
                cos, sin = cos_ref[k : k + 1, :], sin_ref[k : k + 1, :]
                to = pl.ds(pl.multiple_of((k % k1l) * x_local + i * 8, 8), 8)
                left = (k // k1l) * 2 * LANES
                x_ref[to, left : left + LANES] = re[k] * cos + im[k] * sin
                x_ref[to, left + LANES : left + 2 * LANES] = im[k] * cos - re[k] * sin

        part = min(rows, 256)

        @pl.loop(0, rows // part)
        def _(j):
            at = pl.ds(pl.multiple_of(j * part, part), part)
            out_ref[:, at] = dot3(split(table_ref[...]), split(x_ref[at]), NT)

    (out,) = call(
        kernel,
        "project",
        [shape((table.shape[0], rows))],
        [bounds, rc, payload, table, tw_cos, tw_sin],
        scratch=[
            pltpu.VMEM((2 * half, chunk), BF16),
            pltpu.VMEM((2 * half, grid_y + FIRST), F32),
            pltpu.VMEM((rows, width), F32),
        ],
        smem_in=(0,),
        far=(1, 2, 3, 4, 5),
        flops=4 * half * slots * grid_y,
    )
    return out


def spectral_call(data, kernel_t, fwd, inv, tw_cos, tw_sin, devices, after):
    lanes = data.shape[1]
    rows = data.shape[0] // (2 * devices)

    def kernel(wait, in_ref, kt_ref, fh_ref, fl_ref, ih_ref, il_ref, cos_ref, sin_ref, out_ref, re_ref, im_ref):
        wait(6, 7)

        @pl.loop(0, lanes // LANES)
        def _(t):
            at = pl.ds(pl.multiple_of(t * LANES, LANES), LANES)
            re = [in_ref[(2 * s) * rows : (2 * s + 1) * rows, at] for s in range(devices)]
            im = [in_ref[(2 * s + 1) * rows : (2 * s + 2) * rows, at] for s in range(devices)]
            re, im = fft_list(re, im, -1.0)
            for k in range(devices):
                cos, sin = cos_ref[k : k + 1, at], sin_ref[k : k + 1, at]
                re_ref[k * rows : (k + 1) * rows, at] = re[k] * cos + im[k] * sin
                im_ref[k * rows : (k + 1) * rows, at] = im[k] * cos - re[k] * sin

        wait(1, 2, 3, 4, 5)
        @pl.loop(0, lanes // LANES)
        def _(t):
            at = pl.ds(pl.multiple_of(t * LANES, LANES), LANES)
            both = jnp.concatenate([re_ref[:, at], im_ref[:, at]], axis=1)
            spectrum = dot3(split(both), (fh_ref[...], fl_ref[...]), NN)
            factor = kt_ref[:, at]
            both = jnp.concatenate([spectrum[:, :LANES] * factor, spectrum[:, LANES:] * factor], axis=1)
            back = dot3(split(both), (ih_ref[...], il_ref[...]), NN)
            re_ref[:, at] = back[:, :LANES]
            im_ref[:, at] = back[:, LANES:]

        @pl.loop(0, lanes // LANES)
        def _(t):
            at = pl.ds(pl.multiple_of(t * LANES, LANES), LANES)
            re, im = [], []
            for k in range(devices):
                cos, sin = cos_ref[k : k + 1, at], sin_ref[k : k + 1, at]
                a = re_ref[k * rows : (k + 1) * rows, at]
                b = im_ref[k * rows : (k + 1) * rows, at]
                re.append(a * cos - b * sin)
                im.append(b * cos + a * sin)
            re, im = fft_list(re, im, 1.0)
            for s in range(devices):
                out_ref[(2 * s) * rows : (2 * s + 1) * rows, at] = re[s]
                out_ref[(2 * s + 1) * rows : (2 * s + 2) * rows, at] = im[s]

    (out,) = call(
        kernel,
        "spectral",
        [shape(data.shape)],
        [data, kernel_t, *fwd, *inv, tw_cos, tw_sin],
        scratch=[
            pltpu.VMEM((devices * rows, lanes), F32),
            pltpu.VMEM((devices * rows, lanes), F32),
        ],
        far=(1, 2, 3, 4, 5, 6, 7),
        flops=1 << 30,
        after=after,
    )
    return out


def sample_call(data, bounds, rc, payload, table, tw_cos, tw_sin, x_local, grid_y, after):
    slots = rc.shape[1]
    n1 = grid_y // LANES
    k1l = n1 // HALVES
    rows = k1l * x_local
    width = HALVES * 2 * LANES
    chunks = bounds.shape[1]
    chunk = slots // chunks
    half = 4 * x_local

    def kernel(wait, in_ref, bound_ref, rc_ref, pay_ref, table_ref, cos_ref, sin_ref, out_ref, u_ref, g_ref, p_ref, t_ref):
        part = min(rows, 256)
        wait(4)

        @pl.loop(0, rows // part)
        def _(j):
            at = pl.ds(pl.multiple_of(j * part, part), part)
            u_ref[at] = dot3(split(jnp.transpose(in_ref[:, at])), split(table_ref[...]), NN)

        wait(5, 6)

        @pl.loop(0, x_local // 8)
        def _(i):
            re, im = [], []
            for k in range(n1):
                cos, sin = cos_ref[k : k + 1, :], sin_ref[k : k + 1, :]
                at = pl.ds(pl.multiple_of((k % k1l) * x_local + i * 8, 8), 8)
                left = (k // k1l) * 2 * LANES
                a = u_ref[at, left : left + LANES]
                b = u_ref[at, left + LANES : left + 2 * LANES]
                re.append(a * cos - b * sin)
                im.append(b * cos + a * sin)
            re, im = fft_list(re, im, 1.0)
            re_at = pl.ds(pl.multiple_of(i * 8, 8), 8)
            im_at = pl.ds(pl.multiple_of(x_local + i * 8, 8), 8)
            for y in range(n1):
                g_ref[re_at, y * LANES : (y + 1) * LANES] = re[y]
                g_ref[im_at, y * LANES : (y + 1) * LANES] = im[y]

        @pl.loop(0, x_local // 8)
        def _(i):
            at = pl.ds(pl.multiple_of(i * 16, 16), 16)
            for b in range(2):
                value = g_ref[at] if b == 0 else pltpu.roll(g_ref[at], grid_y - 1, 1)
                hi, lo = split(value)
                base = 2 * b * x_local
                p_ref[pl.ds(pl.multiple_of(base + i * 16, 16), 16), :grid_y] = hi
                p_ref[pl.ds(pl.multiple_of(half + base + i * 16, 16), 16), :grid_y] = lo

        p_ref[:, grid_y:] = jnp.zeros((2 * half, FIRST), BF16)
        out_ref[...] = jnp.zeros(out_ref.shape, F32)
        wait(2, 3)

        @pl.loop(0, chunks)
        def _(i):
            @pl.when(bound_ref[1, i] >= 0)
            def _():
                at = pl.ds(pl.multiple_of(i * chunk, chunk), chunk)

                col = rc_ref[1:2, at]

                def visit(start, size):
                    part = dot(p_ref[:, pl.ds(start, size)], one_hot(col, start, size), NN)
                    t_ref[...] = part if size == FIRST else t_ref[...] + part

                visit_windows(bound_ref, i, visit)
                @pl.loop(0, chunk // 256)
                def _(j):
                    at = pl.ds(pl.multiple_of(i * chunk + j * 256, 256), 256)
                    of = pl.ds(pl.multiple_of(j * 256, 256), 256)
                    ids = lax.broadcasted_iota(jnp.int32, (x_local, 256), 0)
                    m0 = ids == rc_ref[0:1, at]
                    m1 = ids == rc_ref[0:1, at] + 1
                    for c in range(2):
                        result = jnp.zeros((x_local, 256), F32)
                        for b in range(2):
                            other = 10 - 4 * c
                            w0 = pay_ref[other + b : other + b + 1, at]
                            w1 = pay_ref[other + 2 + b : other + 3 + b, at]
                            base = (b * 2 + c) * x_local
                            weight = jnp.where(m0, w0, jnp.where(m1, w1, 0.0))
                            low = t_ref[base : base + x_local, of]
                            high = t_ref[half + base : half + base + x_local, of]
                            result = result + weight * (low + high)
                        out_ref[c : c + 1, at] = jnp.sum(result, axis=0, keepdims=True)

    (out,) = call(
        kernel,
        "sample",
        [shape((2, slots))],
        [data, bounds, rc, payload, table, tw_cos, tw_sin],
        scratch=[
            pltpu.VMEM((rows, width), F32),
            pltpu.VMEM((2 * x_local, grid_y), F32),
            pltpu.VMEM((2 * half, grid_y + FIRST), BF16),
            pltpu.VMEM((2 * half, chunk), F32),
        ],
        smem_in=(1,),
        far=(2, 3, 4, 5, 6),
        flops=4 * half * slots * grid_y,
        after=after,
    )
    return out


def split_outside(x):
    hi = lax.reduce_precision(x, 8, 7)
    return hi.astype(BF16), (x - hi).astype(BF16)


def near_terms(currents, probes, near_list, near_matrix):
    block_len = near_matrix.shape[2]
    blocks = near_list.shape[0]
    select = (near_list[:, :, None] == jnp.arange(blocks, dtype=jnp.int32)[None, None, :]).astype(F32)
    cur_blocks = currents.reshape(3, blocks, block_len)
    gathered = jnp.einsum("ctj,bnt->cbnj", cur_blocks, select, precision=lax.Precision.HIGHEST)
    g_hi, g_lo = split_outside(gathered)
    forward = jnp.einsum(
        "cbnj,bnij->cbi", jnp.concatenate([g_hi, g_lo]), near_matrix, preferred_element_type=F32
    )
    p_hi, p_lo = split_outside(probes.reshape(3, blocks, block_len))
    spread = jnp.einsum(
        "cbi,bnij->cbnj", jnp.concatenate([p_hi, p_lo]), near_matrix, preferred_element_type=F32
    )
    adjoint = jnp.einsum(
        "cbnj,bnt->ctj", spread[:3] + spread[3:], select, precision=lax.Precision.HIGHEST
    )
    return (forward[:3] + forward[3:]).reshape(3, -1), adjoint.reshape(3, -1)


def on_device(
    currents, probes, proj_weights, interp_weights, owner, cell, near_list, near_matrix, kernel_hat
):
    devices = lax.axis_size("row") * lax.axis_size("col")
    elem_count = currents.shape[1]
    capacity = 2 * elem_count // devices
    dz_count, ky_local, grid_x = kernel_hat.shape
    assert dz_count == 1
    grid_y = ky_local * devices
    x_local = grid_x // devices
    slots = devices * capacity
    n1 = grid_y // LANES
    per = ky_local // n1
    k1l = n1 // HALVES

    codes = x_local * grid_y
    assert codes & (codes - 1) == 0

    target = owner[:, 0]
    row, col = cell // grid_y % (x_local - 1), cell % grid_y
    key = target * codes + col * x_local + row
    columns = [*currents, *probes, *proj_weights, *interp_weights]
    order = lax.iota(jnp.int32, elem_count)
    key, *columns, order = lax.sort((key, *columns, order), num_keys=1, is_stable=False)
    bounds_of = jnp.arange(devices + 1, dtype=jnp.int32)
    starts = jnp.sum((target[None, :] < bounds_of[:, None]).astype(jnp.int32), axis=1)
    outgoing = expand_call(
        starts, key[None, :], [x[None, :] for x in columns], devices, capacity, codes
    )
    arrived = lax.all_to_all(outgoing, AXES, split_axis=0, concat_axis=0, tiled=True)
    payload, rc, bounds, held = gather_groups(arrived, x_local, CHUNK)

    table = jnp.asarray(y_table(devices, per), F32)
    ty_cos, ty_sin = (jnp.asarray(t, F32) for t in phases(n1, LANES, grid_y))
    tx_cos, tx_sin = (
        jnp.asarray(np.tile(t, (1, k1l)), F32) for t in phases(devices, x_local, grid_x)
    )
    fwd, inv = split_np(x_table(x_local, -1.0)), split_np(x_table(x_local, 1.0))

    kernel_view = kernel_hat.reshape(per, HALVES, k1l, x_local, devices)
    kernel_t = jnp.transpose(kernel_view, (4, 1, 0, 2, 3)) * (1.0 / (grid_x * grid_y))
    kernel_t = kernel_t.reshape(devices * HALVES * per, k1l * x_local)

    def exchange(*fields):
        shaped = [x.reshape(devices, -1, x.shape[1]) for x in fields]
        height = shaped[0].shape[1]
        moved = lax.all_to_all(
            jnp.concatenate(shaped, axis=1), AXES, split_axis=0, concat_axis=0, tiled=True
        )
        parts = [moved[:, i * height : (i + 1) * height] for i in range(len(fields))]
        return [x.reshape(fields[0].shape) for x in parts]

    def spectral(spectra, *after):
        return spectral_call(spectra, kernel_t, fwd, inv, tx_cos, tx_sin, devices, after)

    def sample(products, *after):
        return sample_call(
            products, bounds, rc, payload, table, ty_cos, ty_sin, x_local, grid_y, after
        )

    spectra = []
    for field in range(3):
        grids = project_call(field, bounds, rc, payload, table, ty_cos, ty_sin, x_local, grid_y)
        spectra.extend(exchange(grids))
    products = exchange(spectral(spectra[0]), spectral(spectra[1]))
    products += exchange(spectral(spectra[2]))
    first = sample(products[0])
    second = sample(products[1])
    third = sample(products[2], first, second)
    results = [first, second, third]
    returning = scatter_groups(jnp.concatenate(results, axis=0), held, devices, capacity)
    returned = lax.all_to_all(returning, AXES, split_axis=0, concat_axis=0, tiled=True)
    homed = compact_call(starts, returned, elem_count)
    _, *homed = lax.sort((order, *homed), num_keys=1, is_stable=False)
    near_forward, near_adjoint = near_terms(currents, probes, near_list, near_matrix)
    return (jnp.stack(homed[0::2]) + near_forward, jnp.stack(homed[1::2]) + near_adjoint)


def solution(mesh):
    return jax.shard_map(
        on_device,
        mesh=mesh,
        in_specs=(
            P(None, AXES),
            P(None, AXES),
            P(None, AXES),
            P(None, AXES),
            P(AXES, None),
            P(AXES),
            P(AXES, None),
            P(AXES, None, None, None),
            P(None, AXES, None),
        ),
        out_specs=(P(None, AXES), P(None, AXES)),
        check_vma=False,
    )
```

```python
import math

import jax
import jax.numpy as jnp
import numpy as np
from jax import lax
from jax.experimental import pallas as pl
from jax.experimental.pallas import tpu as pltpu
from jax.sharding import PartitionSpec as P

AXES = ("row", "col")
LANES = 128
HALVES = 2
GROUP = 8
CHUNK = 1024
FIRST = 768
WINDOW = 256
F32 = jnp.float32
BF16 = jnp.bfloat16
NT = (((1,), (1,)), ((), ()))
NN = (((1,), (0,)), ((), ()))


def split_np(table):
    hi = table.astype(np.float32).astype(jnp.bfloat16)
    lo = (table - hi.astype(np.float64)).astype(np.float32).astype(jnp.bfloat16)
    return jnp.asarray(hi), jnp.asarray(lo)


def split(x):
    hi = x.astype(BF16)
    return hi, (x - hi.astype(F32)).astype(BF16)


def dot(a, b, dims):
    return lax.dot_general(a, b, dims, preferred_element_type=F32)


def dot3(a, b, dims):
    (ah, al), (bh, bl) = a, b
    return dot(ah, bh, dims) + (dot(ah, bl, dims) + dot(al, bh, dims))


def y_table(devices, per):
    d, c, h, q, hh, cc, y = np.ix_(
        range(devices), range(2), range(HALVES), range(per), range(HALVES), range(2), range(LANES)
    )
    angle = 2.0 * math.pi * (((d * per + q) * y) % LANES) / LANES
    sine = np.where(c < cc, 1.0, -1.0) * np.sin(angle)
    value = np.where(c == cc, np.cos(angle), sine) * (h == hh)
    return value.reshape(devices * 2 * HALVES * per, HALVES * 2 * LANES)


def x_table(length, direction):
    copies = LANES // length
    c, p, x, cc, pp, k = np.ix_(
        range(2), range(copies), range(length), range(2), range(copies), range(length)
    )
    angle = direction * 2.0 * math.pi * ((x * k) % length) / length
    sine = np.where(c < cc, 1.0, -1.0) * np.sin(angle)
    value = np.where(c == cc, np.cos(angle), sine) * (p == pp)
    return value.reshape(2 * LANES, 2 * LANES)


def phases(rows, cols, length):
    turns = (np.arange(rows)[:, None] * np.arange(cols)[None, :]) % length
    angle = 2.0 * math.pi * turns / length
    return np.cos(angle), np.sin(angle)


def fft_list(re, im, direction):
    n = len(re)
    if n == 1:
        return re, im
    even_re, even_im = fft_list(re[0::2], im[0::2], direction)
    odd_re, odd_im = fft_list(re[1::2], im[1::2], direction)
    low_re, low_im, high_re, high_im = [], [], [], []
    for k in range(n // 2):
        a, b = odd_re[k], odd_im[k]
        if k == 0:
            tr, ti = a, b
        elif 4 * k == n:
            tr, ti = (-b, a) if direction > 0 else (b, -a)
        else:
            cos = math.cos(2.0 * math.pi * k / n)
            sin = direction * math.sin(2.0 * math.pi * k / n)
            tr, ti = a * cos - b * sin, a * sin + b * cos
        low_re.append(even_re[k] + tr)
        low_im.append(even_im[k] + ti)
        high_re.append(even_re[k] - tr)
        high_im.append(even_im[k] - ti)
    return low_re + high_re, low_im + high_im


def one_hot(cols, start, size):
    ids = lax.broadcasted_iota(jnp.int32, (size, cols.shape[1]), 0) + start
    return jnp.where(ids == cols, 1.0, 0.0).astype(BF16)


def call(kernel, name, out_shape, args, scratch=(), smem_in=(), smem_out=(), far=(), flops=0, after=()):
    count, skip, results = len(args), len(after), len(out_shape)
    spaces = [
        pltpu.SMEM if i in smem_in else pl.ANY if i in far else pltpu.VMEM for i in range(count)
    ]
    outs = [pltpu.SMEM if i in smem_out else pltpu.VMEM for i in range(results)]
    moved = sum(math.prod(x.shape) * x.dtype.itemsize for x in (*args, *out_shape))
    near_by = [pltpu.VMEM(args[i].shape, args[i].dtype) for i in far]
    sems = [pltpu.SemaphoreType.DMA((len(far),))] if far else []

    def body(*refs):
        refs = refs[:count] + refs[count + skip :]
        if not far:
            return kernel(*refs)
        refs, targets, sem = list(refs[: -len(far) - 1]), refs[-len(far) - 1 : -1], refs[-1]
        copies = {}
        for j, i in enumerate(far):
            copies[i] = pltpu.make_async_copy(refs[i], targets[j], sem.at[j])
            copies[i].start()
            refs[i] = targets[j]

        def wait(*numbers):
            for i in numbers:
                copies[i].wait()

        return kernel(wait, *refs)

    return pl.pallas_call(
        body,
        out_shape=list(out_shape),
        in_specs=[pl.BlockSpec(memory_space=space) for space in spaces]
        + [pl.BlockSpec(memory_space=pl.ANY)] * skip,
        out_specs=[pl.BlockSpec(memory_space=space) for space in outs],
        scratch_shapes=[*scratch, *near_by, *sems],
        compiler_params=pltpu.CompilerParams(vmem_limit_bytes=32 << 20),
        cost_estimate=pl.CostEstimate(flops=flops, transcendentals=0, bytes_accessed=moved),
        name=name,
    )(*args, *after)


def shape(dims, dtype=F32):
    return jax.ShapeDtypeStruct(dims, dtype)


def rows_call(arrays):
    count = arrays[0].shape[1]
    spots = [(n, r) for n, x in enumerate(arrays) for r in range(x.shape[0])]

    def kernel(wait, *refs):
        wait(*range(len(arrays)))
        for (n, r), out_ref in zip(spots, refs[len(arrays) :]):
            for k in range(count // LANES):
                out_ref[k : k + 1] = refs[n][r : r + 1, k * LANES : (k + 1) * LANES]

    outs = [shape((count // LANES, LANES))] * len(spots)
    rows = call(kernel, "rows", outs, arrays, far=tuple(range(len(arrays))))
    return [x.reshape(count) for x in rows]


def expand_call(starts, keys, rows, devices, capacity, codes):
    count = keys.shape[1]
    wide = -(-capacity // LANES) * LANES + LANES
    height = 16

    def kernel(starts_ref, key_ref, *refs):
        row_refs, out_ref, s_ref = refs[:-2], refs[-2], refs[-1]
        s_ref[:, count:] = jnp.zeros((height, wide), F32)
        for i, ref in enumerate(row_refs):
            s_ref[i : i + 1, 0:count] = ref[...]
        s_ref[height - 1 : height, 0:count] = (key_ref[...] & (codes - 1)).astype(F32)
        lane = lax.broadcasted_iota(jnp.int32, (height, wide), 1)
        rank = lax.broadcasted_iota(jnp.int32, (height, wide), 0)
        free = jnp.where(rank == height - 1, -1.0, 0.0)

        @pl.loop(0, devices, unroll=4)
        def _(d):
            first = starts_ref[d]
            held = starts_ref[d + 1] - first
            tile = first // LANES
            block = s_ref[:, pl.ds(pl.multiple_of(tile * LANES, LANES), wide)]
            moved = pltpu.roll(block, wide - (first - tile * LANES), 1)
            kept = jnp.where(lane < held, moved, free)
            out_ref[d] = jnp.where(rank == height - 2, held.astype(F32), kept)[:, :capacity]

    (out,) = call(
        kernel,
        "expand",
        [shape((devices, height, capacity))],
        [starts, keys, *rows],
        scratch=[pltpu.VMEM((height, count + wide), F32)],
        smem_in=(0,),
    )
    return out


def compact_call(starts, data, count):
    devices, height, capacity = data.shape
    wide = -(-capacity // LANES) * LANES + LANES

    def kernel(starts_ref, in_ref, out_ref, s_ref, r_ref):
        lane = lax.broadcasted_iota(jnp.int32, (height, wide), 1)
        filler = jnp.zeros((height, wide - capacity), F32)

        @pl.loop(0, devices, unroll=4)
        def _(d):
            whole = jnp.concatenate([in_ref[d], filler], axis=1)
            r_ref[d] = pltpu.roll(whole, starts_ref[d] % LANES, 1)

        @pl.loop(0, devices)
        def _(d):
            first = starts_ref[d]
            shift = first % LANES
            left = pl.multiple_of(first - shift, LANES)
            edge = jnp.where(lane[:, :LANES] < shift, s_ref[:, pl.ds(left, LANES)], r_ref[d, :, :LANES])
            s_ref[:, pl.ds(left, LANES)] = edge
            s_ref[:, pl.ds(left + LANES, wide - LANES)] = r_ref[d, :, LANES:]

        out_ref[...] = s_ref[:, :count]

    (out,) = call(
        kernel,
        "compact",
        [shape((height, count))],
        [starts, data],
        scratch=[
            pltpu.VMEM((height, count + wide), F32),
            pltpu.VMEM((devices, height, wide), F32),
        ],
        smem_in=(0,),
    )
    return out


def turn_blocks(parts):
    parts = list(parts)
    block = lax.broadcasted_iota(jnp.int32, parts[0].shape, 1) // GROUP
    for m in (1, 2, 4, 8):
        high = (block & m) != 0
        for i in range(16):
            if i & m == 0:
                a, b = parts[i], parts[i + m]
                parts[i] = jnp.where(high, pltpu.roll(b, m * GROUP, 1), a)
                parts[i + m] = jnp.where(high, b, pltpu.roll(a, LANES - m * GROUP, 1))
    return parts


def pick_lanes(tiles, place):
    dims = tiles[0].shape
    index = jnp.broadcast_to(jnp.clip(place, 0.0, len(tiles) * LANES - 1.0).astype(jnp.int32), dims)
    result = None
    for k, tile in enumerate(tiles):
        part = jnp.take_along_axis(tile, index & (LANES - 1), axis=1)
        result = part if k == 0 else jnp.where(index < k * LANES, result, part)
    return result


def gather_groups(arrived, x_local, chunk):
    devices, height, capacity = arrived.shape
    slots = devices * capacity
    chunks = slots // chunk
    shift = x_local.bit_length() - 1
    none = 1 << 20

    def decode(code):
        return code & (x_local - 1), lax.shift_right_arithmetic(code, shift)

    if capacity % LANES or devices % 16:
        turned = arrived.reshape(devices, height, capacity // GROUP, GROUP)
        turned = jnp.transpose(turned, (1, 2, 0, 3)).reshape(height, slots)
        row, col = decode(turned[height - 1].astype(jnp.int32))
        per_chunk = col.reshape(chunks, chunk)
        low = jnp.min(jnp.where(per_chunk < 0, none, per_chunk), axis=1)
        bounds = jnp.stack([low, jnp.max(per_chunk, axis=1)])
        return turned, jnp.stack([row, col]), bounds, jnp.zeros((8, LANES), F32)

    tiles = capacity // LANES

    def kernel(in_ref, out_ref, rc_ref, bound_ref, held_ref):
        most = jnp.zeros((1, LANES), F32)
        for i in range(devices):
            held = in_ref[i, height - 2 : height - 1, :LANES]
            held_ref[i : i + 1] = held
            most = jnp.maximum(most, held)
        held_ref[devices:] = jnp.broadcast_to(most, (8, LANES))
        per = 1.0 / jnp.maximum(most, 1.0)
        lane = lax.broadcasted_iota(jnp.int32, (1, LANES), 1).astype(F32)
        rank = lax.broadcasted_iota(jnp.int32, (height, LANES), 0)
        free = jnp.where(rank == height - 1, -1.0, 0.0)

        @pl.loop(0, devices // 16 * tiles)
        def _(n):
            sb, t = n // tiles, n % tiles
            slot = lane + (t * LANES).astype(F32)
            parts = []
            for i in range(16):
                sender = sb * 16 + i
                held = in_ref[sender, height - 2 : height - 1, :LANES]
                place = jnp.floor((slot * held + 0.5) * per)
                before = jnp.floor(((slot - 1.0) * held + 0.5) * per)
                valid = (place > before) & (slot < most)
                across = [in_ref[sender, :, k * LANES : (k + 1) * LANES] for k in range(tiles)]
                parts.append(jnp.where(valid, pick_lanes(across, place), free))
            for j, part in enumerate(turn_blocks(parts)):
                left = (t * 16 + j) * devices * GROUP + sb * LANES
                at = pl.ds(pl.multiple_of(left, LANES), LANES)
                out_ref[:, at] = part
                row, col = decode(part[height - 1 :].astype(jnp.int32))
                rc_ref[0:1, at] = row
                rc_ref[1:2, at] = col

        @pl.loop(0, chunks)
        def _(i):
            col = rc_ref[1:2, pl.ds(pl.multiple_of(i * chunk, chunk), chunk)]
            bound_ref[0, i] = jnp.min(jnp.where(col < 0, none, col))
            bound_ref[1, i] = jnp.max(col)

    return call(
        kernel,
        "groups",
        [
            shape((height, slots)),
            shape((2, slots), jnp.int32),
            shape((2, chunks), jnp.int32),
            shape((devices + 8, LANES)),
        ],
        [arrived],
        smem_out=(2,),
    )


def scatter_groups(results, held, devices, capacity):
    height = results.shape[0]
    if capacity % LANES or devices % 16:
        turned = results.reshape(height, capacity // GROUP, devices, GROUP)
        return jnp.transpose(turned, (2, 0, 1, 3)).reshape(devices, height, capacity)

    tiles = capacity // LANES

    def kernel(in_ref, held_ref, out_ref):
        most = held_ref[devices : devices + 1]
        lane = lax.broadcasted_iota(jnp.int32, (1, LANES), 1).astype(F32)

        @pl.loop(0, devices // 16)
        def _(sb):
            turned = []
            for t in range(tiles):
                parts = []
                for j in range(16):
                    left = (t * 16 + j) * devices * GROUP
                    parts.append(in_ref[:, pl.ds(pl.multiple_of(left + sb * LANES, LANES), LANES)])
                turned.append(turn_blocks(parts))
            for i in range(16):
                sender = sb * 16 + i
                here = jnp.maximum(held_ref[pl.ds(sender, 1)], 1.0)
                for t in range(tiles):
                    place = jnp.floor(((lane + t * LANES) * most + here - 0.5) / here)
                    picked = pick_lanes([turned[k][i] for k in range(tiles)], place)
                    out_ref[sender, :, t * LANES : (t + 1) * LANES] = picked

    (out,) = call(kernel, "ungroup", [shape((devices, height, capacity))], [results, held])
    return out


def y_phase(table_ref, k, n1):
    lanes = slice(k % 4 * LANES, k % 4 * LANES + LANES)
    cos, sin = 4 * LANES + k // 4, 4 * LANES + (n1 + k) // 4
    return table_ref[cos : cos + 1, lanes], table_ref[sin : sin + 1, lanes]


def visit_windows(bound_ref, i, visit):
    first = pl.multiple_of(bound_ref[0, i] // LANES * LANES, LANES)
    visit(first, FIRST)

    def step(w, carry):
        visit(pl.multiple_of(first + FIRST + w * WINDOW, LANES), WINDOW)
        return carry

    lax.fori_loop(0, (bound_ref[1, i] - first - FIRST) // WINDOW + 1, step, 0)


def project_call(field, bounds, rc, payload, table, x_local, grid_y):
    slots = rc.shape[1]
    chunks = bounds.shape[1]
    chunk = slots // chunks
    n1 = grid_y // LANES
    k1l = n1 // HALVES
    rows = k1l * x_local
    width = HALVES * 2 * LANES
    half = 4 * x_local
    height = 4 * LANES

    def kernel(wait, bound_ref, rc_ref, pay_ref, table_ref, out_ref, v_ref, acc_ref, x_ref):
        @pl.loop(0, half // 32)
        def _(i):
            acc_ref[pl.ds(pl.multiple_of(i * 64, 64), 64)] = jnp.zeros((64, acc_ref.shape[1]), F32)

        wait(1, 2)

        @pl.loop(0, chunks)
        def _(i):
            @pl.when(bound_ref[1, i] >= 0)
            def _():
                @pl.loop(0, chunk // 512)
                def _(j):
                    at = pl.ds(pl.multiple_of(i * chunk + j * 512, 512), 512)
                    to = pl.ds(pl.multiple_of(j * 512, 512), 512)
                    ids = lax.broadcasted_iota(jnp.int32, (x_local, 512), 0)
                    m0 = ids == rc_ref[0:1, at]
                    m1 = ids == rc_ref[0:1, at] + 1
                    for c in range(2):
                        u = pay_ref[3 * c + field : 3 * c + field + 1, at]
                        for b in range(2):
                            p0 = u * pay_ref[6 + 4 * c + b : 7 + 4 * c + b, at]
                            p1 = u * pay_ref[8 + 4 * c + b : 9 + 4 * c + b, at]
                            hi, lo = split(jnp.where(m0, p0, jnp.where(m1, p1, 0.0)))
                            base = (b * 2 + c) * x_local
                            v_ref[base : base + x_local, to] = hi
                            v_ref[half + base : half + base + x_local, to] = lo

                col = rc_ref[1:2, pl.ds(pl.multiple_of(i * chunk, chunk), chunk)]

                def visit(start, size):
                    acc_ref[:, pl.ds(start, size)] += dot(v_ref[...], one_hot(col, start, size), NT)

                visit_windows(bound_ref, i, visit)

        wait(3)

        @pl.loop(0, x_local // 8)
        def _(i):
            def rows_of(base):
                low = pl.ds(pl.multiple_of(base + i * 8, 8), 8)
                high = pl.ds(pl.multiple_of(half + base + i * 8, 8), 8)
                return acc_ref[low, :grid_y] + acc_ref[high, :grid_y]

            parts = []
            for c in range(2):
                g = rows_of(c * x_local) + pltpu.roll(rows_of((2 + c) * x_local), 1, 1)
                parts.append([g[:, y * LANES : (y + 1) * LANES] for y in range(n1)])
            re, im = fft_list(parts[0], parts[1], -1.0)
            for k in range(n1):
                cos, sin = y_phase(table_ref, k, n1)
                to = pl.ds(pl.multiple_of((k % k1l) * x_local + i * 8, 8), 8)
                left = (k // k1l) * 2 * LANES
                x_ref[to, left : left + LANES] = re[k] * cos + im[k] * sin
                x_ref[to, left + LANES : left + 2 * LANES] = im[k] * cos - re[k] * sin

        out_ref[...] = dot3(split(table_ref[:height]), split(x_ref[...]), NT)

    (out,) = call(
        kernel,
        "project",
        [shape((height, rows))],
        [bounds, rc, payload, table],
        scratch=[
            pltpu.VMEM((2 * half, chunk), BF16),
            pltpu.VMEM((2 * half, grid_y + FIRST), F32),
            pltpu.VMEM((rows, width), F32),
        ],
        smem_in=(0,),
        far=(1, 2, 3),
        flops=4 * half * slots * grid_y,
    )
    return out


def spectral_call(data, kernel_t, fwd, inv, tw_cos, tw_sin, devices, after):
    lanes = data.shape[1]
    rows = data.shape[0] // (2 * devices)

    def kernel(wait, in_ref, kt_ref, fh_ref, fl_ref, ih_ref, il_ref, cos_ref, sin_ref, out_ref, re_ref, im_ref):
        wait(6, 7)

        @pl.loop(0, lanes // LANES)
        def _(t):
            at = pl.ds(pl.multiple_of(t * LANES, LANES), LANES)
            re = [in_ref[(2 * s) * rows : (2 * s + 1) * rows, at] for s in range(devices)]
            im = [in_ref[(2 * s + 1) * rows : (2 * s + 2) * rows, at] for s in range(devices)]
            re, im = fft_list(re, im, -1.0)
            for k in range(devices):
                cos, sin = cos_ref[k : k + 1, at], sin_ref[k : k + 1, at]
                re_ref[k * rows : (k + 1) * rows, at] = re[k] * cos + im[k] * sin
                im_ref[k * rows : (k + 1) * rows, at] = im[k] * cos - re[k] * sin

        wait(1, 2, 3, 4, 5)
        @pl.loop(0, lanes // LANES)
        def _(t):
            at = pl.ds(pl.multiple_of(t * LANES, LANES), LANES)
            both = jnp.concatenate([re_ref[:, at], im_ref[:, at]], axis=1)
            spectrum = dot3(split(both), (fh_ref[...], fl_ref[...]), NN)
            factor = kt_ref[:, at]
            both = jnp.concatenate([spectrum[:, :LANES] * factor, spectrum[:, LANES:] * factor], axis=1)
            back = dot3(split(both), (ih_ref[...], il_ref[...]), NN)
            re_ref[:, at] = back[:, :LANES]
            im_ref[:, at] = back[:, LANES:]

        @pl.loop(0, lanes // LANES)
        def _(t):
            at = pl.ds(pl.multiple_of(t * LANES, LANES), LANES)
            re, im = [], []
            for k in range(devices):
                cos, sin = cos_ref[k : k + 1, at], sin_ref[k : k + 1, at]
                a = re_ref[k * rows : (k + 1) * rows, at]
                b = im_ref[k * rows : (k + 1) * rows, at]
                re.append(a * cos - b * sin)
                im.append(b * cos + a * sin)
            re, im = fft_list(re, im, 1.0)
            for s in range(devices):
                out_ref[(2 * s) * rows : (2 * s + 1) * rows, at] = re[s]
                out_ref[(2 * s + 1) * rows : (2 * s + 2) * rows, at] = im[s]

    (out,) = call(
        kernel,
        "spectral",
        [shape(data.shape)],
        [data, kernel_t, *fwd, *inv, tw_cos, tw_sin],
        scratch=[
            pltpu.VMEM((devices * rows, lanes), F32),
            pltpu.VMEM((devices * rows, lanes), F32),
        ],
        far=(1, 2, 3, 4, 5, 6, 7),
        flops=1 << 30,
        after=after,
    )
    return out


def sample_call(data, bounds, rc, payload, table, x_local, grid_y, after):
    slots = rc.shape[1]
    n1 = grid_y // LANES
    k1l = n1 // HALVES
    rows = k1l * x_local
    width = HALVES * 2 * LANES
    chunks = bounds.shape[1]
    chunk = slots // chunks
    half = 4 * x_local
    height = 4 * LANES

    def kernel(wait, in_ref, bound_ref, rc_ref, pay_ref, table_ref, out_ref, u_ref, g_ref, p_ref, t_ref):
        part = min(rows, 256)
        wait(4)

        @pl.loop(0, rows // part)
        def _(j):
            at = pl.ds(pl.multiple_of(j * part, part), part)
            u_ref[at] = dot3(split(jnp.transpose(in_ref[:, at])), split(table_ref[:height]), NN)

        @pl.loop(0, x_local // 8)
        def _(i):
            re, im = [], []
            for k in range(n1):
                cos, sin = y_phase(table_ref, k, n1)
                at = pl.ds(pl.multiple_of((k % k1l) * x_local + i * 8, 8), 8)
                left = (k // k1l) * 2 * LANES
                a = u_ref[at, left : left + LANES]
                b = u_ref[at, left + LANES : left + 2 * LANES]
                re.append(a * cos - b * sin)
                im.append(b * cos + a * sin)
            re, im = fft_list(re, im, 1.0)
            re_at = pl.ds(pl.multiple_of(i * 8, 8), 8)
            im_at = pl.ds(pl.multiple_of(x_local + i * 8, 8), 8)
            for y in range(n1):
                g_ref[re_at, y * LANES : (y + 1) * LANES] = re[y]
                g_ref[im_at, y * LANES : (y + 1) * LANES] = im[y]

        @pl.loop(0, x_local // 8)
        def _(i):
            at = pl.ds(pl.multiple_of(i * 16, 16), 16)
            for b in range(2):
                value = g_ref[at] if b == 0 else pltpu.roll(g_ref[at], grid_y - 1, 1)
                hi, lo = split(value)
                base = 2 * b * x_local
                p_ref[pl.ds(pl.multiple_of(base + i * 16, 16), 16), :grid_y] = hi
                p_ref[pl.ds(pl.multiple_of(half + base + i * 16, 16), 16), :grid_y] = lo

        p_ref[:, grid_y:] = jnp.zeros((2 * half, FIRST), BF16)
        out_ref[...] = jnp.zeros(out_ref.shape, F32)
        wait(2, 3)

        @pl.loop(0, chunks)
        def _(i):
            @pl.when(bound_ref[1, i] >= 0)
            def _():
                at = pl.ds(pl.multiple_of(i * chunk, chunk), chunk)

                col = rc_ref[1:2, at]

                def visit(start, size):
                    part = dot(p_ref[:, pl.ds(start, size)], one_hot(col, start, size), NN)
                    t_ref[...] = part if size == FIRST else t_ref[...] + part

                visit_windows(bound_ref, i, visit)
                @pl.loop(0, chunk // 256)
                def _(j):
                    at = pl.ds(pl.multiple_of(i * chunk + j * 256, 256), 256)
                    of = pl.ds(pl.multiple_of(j * 256, 256), 256)
                    ids = lax.broadcasted_iota(jnp.int32, (x_local, 256), 0)
                    m0 = ids == rc_ref[0:1, at]
                    m1 = ids == rc_ref[0:1, at] + 1
                    for c in range(2):
                        result = jnp.zeros((x_local, 256), F32)
                        for b in range(2):
                            other = 10 - 4 * c
                            w0 = pay_ref[other + b : other + b + 1, at]
                            w1 = pay_ref[other + 2 + b : other + 3 + b, at]
                            base = (b * 2 + c) * x_local
                            weight = jnp.where(m0, w0, jnp.where(m1, w1, 0.0))
                            low = t_ref[base : base + x_local, of]
                            high = t_ref[half + base : half + base + x_local, of]
                            result = result + weight * (low + high)
                        out_ref[c : c + 1, at] = jnp.sum(result, axis=0, keepdims=True)

    (out,) = call(
        kernel,
        "sample",
        [shape((2, slots))],
        [data, bounds, rc, payload, table],
        scratch=[
            pltpu.VMEM((rows, width), F32),
            pltpu.VMEM((2 * x_local, grid_y), F32),
            pltpu.VMEM((2 * half, grid_y + FIRST), BF16),
            pltpu.VMEM((2 * half, chunk), F32),
        ],
        smem_in=(1,),
        far=(2, 3, 4),
        flops=4 * half * slots * grid_y,
        after=after,
    )
    return out


def split_outside(x):
    hi = lax.reduce_precision(x, 8, 7)
    return hi.astype(BF16), (x - hi).astype(BF16)


def near_terms(currents, probes, near_list, near_matrix):
    block_len = near_matrix.shape[2]
    blocks = near_list.shape[0]
    select = (near_list[:, :, None] == jnp.arange(blocks, dtype=jnp.int32)[None, None, :]).astype(F32)
    cur_blocks = currents.reshape(3, blocks, block_len)
    gathered = jnp.einsum("ctj,bnt->cbnj", cur_blocks, select, precision=lax.Precision.HIGHEST)
    g_hi, g_lo = split_outside(gathered)
    forward = jnp.einsum(
        "cbnj,bnij->cbi", jnp.concatenate([g_hi, g_lo]), near_matrix, preferred_element_type=F32
    )
    p_hi, p_lo = split_outside(probes.reshape(3, blocks, block_len))
    spread = jnp.einsum(
        "cbi,bnij->cbnj", jnp.concatenate([p_hi, p_lo]), near_matrix, preferred_element_type=F32
    )
    adjoint = jnp.einsum(
        "cbnj,bnt->ctj", spread[:3] + spread[3:], select, precision=lax.Precision.HIGHEST
    )
    return (forward[:3] + forward[3:]).reshape(3, -1), adjoint.reshape(3, -1)


def on_device(
    currents, probes, proj_weights, interp_weights, owner, cell, near_list, near_matrix, kernel_hat
):
    devices = lax.axis_size("row") * lax.axis_size("col")
    elem_count = currents.shape[1]
    capacity = 2 * elem_count // devices
    dz_count, ky_local, grid_x = kernel_hat.shape
    assert dz_count == 1
    grid_y = ky_local * devices
    x_local = grid_x // devices
    slots = devices * capacity
    n1 = grid_y // LANES
    per = ky_local // n1
    k1l = n1 // HALVES

    codes = x_local * grid_y
    assert codes & (codes - 1) == 0

    target = owner[:, 0]
    row, col = cell // grid_y % (x_local - 1), cell % grid_y
    key = target * codes + col * x_local + row
    columns = rows_call([currents, probes, proj_weights, interp_weights])
    order = lax.iota(jnp.int32, elem_count)
    key, *columns, order = lax.sort((key, *columns, order), num_keys=1, is_stable=False)
    bounds_of = jnp.arange(devices + 1, dtype=jnp.int32)
    starts = jnp.sum((target[None, :] < bounds_of[:, None]).astype(jnp.int32), axis=1)
    outgoing = expand_call(
        starts, key[None, :], [x[None, :] for x in columns], devices, capacity, codes
    )
    arrived = lax.all_to_all(outgoing, AXES, split_axis=0, concat_axis=0, tiled=True)
    payload, rc, bounds, held = gather_groups(arrived, x_local, CHUNK)

    twiddles = np.concatenate(phases(n1, LANES, grid_y)).reshape(-1, 4 * LANES)
    table = jnp.asarray(np.concatenate([y_table(devices, per), twiddles]), F32)
    tx_cos, tx_sin = (
        jnp.asarray(np.tile(t, (1, k1l)), F32) for t in phases(devices, x_local, grid_x)
    )
    fwd, inv = split_np(x_table(x_local, -1.0)), split_np(x_table(x_local, 1.0))

    kernel_view = kernel_hat.reshape(per, HALVES, k1l, x_local, devices)
    kernel_t = jnp.transpose(kernel_view, (4, 1, 0, 2, 3)) * (1.0 / (grid_x * grid_y))
    kernel_t = kernel_t.reshape(devices * HALVES * per, k1l * x_local)

    def exchange(*fields):
        shaped = [x.reshape(devices, -1, x.shape[1]) for x in fields]
        height = shaped[0].shape[1]
        moved = lax.all_to_all(
            jnp.concatenate(shaped, axis=1), AXES, split_axis=0, concat_axis=0, tiled=True
        )
        parts = [moved[:, i * height : (i + 1) * height] for i in range(len(fields))]
        return [x.reshape(fields[0].shape) for x in parts]

    def spectral(spectra, *after):
        return spectral_call(spectra, kernel_t, fwd, inv, tx_cos, tx_sin, devices, after)

    def sample(products, *after):
        return sample_call(
            products, bounds, rc, payload, table, x_local, grid_y, after
        )

    spectra = []
    for field in range(3):
        grids = project_call(field, bounds, rc, payload, table, x_local, grid_y)
        spectra.extend(exchange(grids))
    products = exchange(spectral(spectra[0]), spectral(spectra[1]))
    products += exchange(spectral(spectra[2]))
    first = sample(products[0])
    second = sample(products[1])
    third = sample(products[2], first, second)
    results = [first, second, third]
    returning = scatter_groups(jnp.concatenate(results, axis=0), held, devices, capacity)
    returned = lax.all_to_all(returning, AXES, split_axis=0, concat_axis=0, tiled=True)
    homed = compact_call(starts, returned, elem_count)
    _, *homed = lax.sort((order, *homed), num_keys=1, is_stable=False)
    near_forward, near_adjoint = near_terms(currents, probes, near_list, near_matrix)
    return (jnp.stack(homed[0::2]) + near_forward, jnp.stack(homed[1::2]) + near_adjoint)


def solution(mesh):
    return jax.shard_map(
        on_device,
        mesh=mesh,
        in_specs=(
            P(None, AXES),
            P(None, AXES),
            P(None, AXES),
            P(None, AXES),
            P(AXES, None),
            P(AXES),
            P(AXES, None),
            P(AXES, None, None, None),
            P(None, AXES, None),
        ),
        out_specs=(P(None, AXES), P(None, AXES)),
        check_vma=False,
    )
```
